32 devices in a mesh: dp: 8 (over z, x), psr: 4 (over y, core).
Axes of the slice: x: 2, y: 2, z: 4, core: 2. Of those that a mesh axis runs over, the one named last changes fastest.
Arguments:
- basis: bfloat16 [32, 4, 8, 128, 256], P(('dp', 'psr')), may hold values from -6 to 6
- residual: bfloat16 [32, 4, 8, 128], P(('dp', 'psr')), may hold values from -6 to 6
- sigma: bfloat16 [32, 4, 8, 128], P(('dp', 'psr')), may hold values from 0.5 to 2
- counts: int32 [32, 4, 8], P(('dp', 'psr')), may hold values from 0 to 128
- pulsar: int32 [32, 4, 8], P(('dp', 'psr')), may hold values from 0 to 3
- ecorr: float32 [16], replicated, may hold values from 0.2 to 2
Outputs:
- gram: float32 [16, 256, 256], P('psr', 'dp')
- rhs: float32 [16, 256], P('psr', 'dp')
- totals: float32 [2], replicated
The draws below stay inside these ranges and needn't reach their ends.
All inputs are finite; a program needn't handle non-finite values.
Results may differ from the reference program's by a relative error of at most 0.0055.
Values may be sent and summed in bfloat16 or wider, within the bound.
A program may use at most 64 MiB of HBM per device.

```python
import math
import jax
import jax.numpy as jnp
from jax import lax

K = 256
L = 128
PG = 4
E_GRP = 8
P_SIZE = 16
SOURCES = 32
NORM_ROWS = 8192
ALL_ROWS = 131072
N_PSR = 4


def plant(entries, stream_key, smallest, top_value):
    index_at = [jax.random.randint(jax.random.fold_in(stream_key, axis), (), 0, length) for axis, length in enumerate(entries.shape)]
    widest = entries.shape.index(max(entries.shape))
    next_to = index_at[:widest] + [(index_at[widest] + 1) % entries.shape[widest]] + index_at[widest + 1:]
    return entries.at[tuple(index_at)].set(smallest).at[tuple(next_to)].set(top_value)


def shard_levels(rng, dims, split, smallest, high):
    def one(axis_at, blocks):
        heights = jax.random.uniform(jax.random.fold_in(jax.random.fold_in(rng, 6), axis_at), (blocks,), jnp.float32, smallest / len(split), high / len(split))
        return jnp.repeat(jnp.exp(heights), dims[axis_at] // blocks).reshape((-1,) + (1,) * (len(dims) - axis_at - 1))

    loudness = one(*split[0])
    for cut in split[1:]:
        loudness = loudness * one(*cut)
    return loudness


def scatter_about(rng, shape, width, reach, shards=(), kind=jnp.bfloat16):
    gain = shard_levels(rng, shape, shards, -0.22, 0.18) if shards else 1.0
    values = jax.random.normal(rng, shape, jnp.float32) * width * gain
    return jnp.minimum(jnp.maximum(values, -reach), reach).astype(kind)


def setup_inputs(seed: int = 0) -> dict:
    seeds = jax.random.split(jax.random.key(seed), 7)
    basis = scatter_about(seeds[0], (SOURCES, N_PSR, E_GRP, L, K), 1.0, 6.0, ((0, 32),))
    residual = scatter_about(seeds[1], (SOURCES, N_PSR, E_GRP, L), 1.0, 6.0, ((0, 32),))
    sigma = jnp.clip(jnp.exp(math.log(2.0) - 1.3862944 * jax.random.uniform(seeds[2], (SOURCES, N_PSR, E_GRP, L), jnp.float32) ** shard_levels(seeds[2], (SOURCES, N_PSR, E_GRP, L), ((0, 32),), -0.2, 0.2)), 0.5, 2.0).astype(jnp.bfloat16)
    counts = plant(jax.random.randint(seeds[3], (SOURCES, N_PSR, E_GRP), 0, L + 1), jax.random.fold_in(seeds[3], 1), 0, L).astype(jnp.int32)
    pulsar = plant(jax.random.randint(seeds[4], (SOURCES, N_PSR, E_GRP), 0, PG), jax.random.fold_in(seeds[4], 1), 0, PG - 1).astype(jnp.int32)
    ecorr = jnp.clip(jnp.exp(jax.random.uniform(seeds[5], (P_SIZE,), jnp.float32, math.log(0.2), math.log(2.0))), 0.2, 2.0)
    return {"basis": basis, "residual": residual, "sigma": sigma, "counts": counts, "pulsar": pulsar, "ecorr": ecorr}


def block_terms(basis, residual, sigma, counts, pulsar, ecorr):
    sig = sigma.astype(jnp.float32)
    res = residual.astype(jnp.float32)
    rowpos = lax.broadcasted_iota(jnp.int32, sig.shape, 2)
    valid = rowpos < counts[..., None]
    inverse = jnp.where(valid, 1.0 / (sig * sig), jnp.float32(0.0))
    weighted = (inverse[..., None] * basis.astype(jnp.float32)).astype(jnp.bfloat16)
    weighted_f = weighted.astype(jnp.float32)
    groups = jnp.arange(N_PSR, dtype=jnp.int32)
    global_id = (groups[:, None] * PG + pulsar).astype(jnp.int32)
    jitter = ecorr[global_id] ** 2
    total = jnp.sum(inverse, axis=2)
    coef = jitter / (1.0 + jitter * total)
    column = jnp.sum(weighted_f, axis=2)
    project = jnp.sum(weighted_f * res[..., None], axis=2)
    wsum = jnp.sum(inverse * res, axis=2)
    chi = jnp.sum(inverse * res * res) - jnp.sum(coef * wsum * wsum)
    logdet = jnp.sum(jnp.where(valid, jnp.log(sig * sig), jnp.float32(0.0))) + jnp.sum(jnp.log(1.0 + jitter * total))
    first = jnp.einsum('gslk,gslm->gskm', basis.astype(jnp.float32), weighted_f, precision=lax.Precision.HIGHEST)
    onehot = (pulsar[..., None] == jnp.arange(PG, dtype=jnp.int32)).astype(jnp.float32)
    gram = jnp.einsum('gsp,gskm->gpkm', onehot, first, precision=lax.Precision.HIGHEST)
    gram = gram - jnp.einsum('gsp,gsk,gsm->gpkm', onehot * coef[..., None], column, column, precision=lax.Precision.HIGHEST)
    rhs = jnp.einsum('gsp,gsk->gpk', onehot, project - (coef * wsum)[..., None] * column, precision=lax.Precision.HIGHEST)
    return gram, rhs, logdet, chi


def reference(basis, residual, sigma, counts, pulsar, ecorr):
    def step(carry, items):
        gram, rhs, logdet, chi = block_terms(items[0], items[1], items[2], items[3], items[4], ecorr)
        return (carry[0] + gram, carry[1] + rhs, carry[2] + logdet, carry[3] + chi), None

    start = (jnp.zeros((N_PSR, PG, K, K), jnp.float32), jnp.zeros((N_PSR, PG, K), jnp.float32), jnp.float32(0.0), jnp.float32(0.0))
    final, _ = lax.scan(step, start, (basis, residual, sigma, counts, pulsar))
    gram = final[0].reshape(P_SIZE, K, K) / NORM_ROWS
    rhs = final[1].reshape(P_SIZE, K) / NORM_ROWS
    totals = jnp.stack([final[2], final[3]]) / ALL_ROWS
    return gram, rhs, totals
```

```python
import functools

import jax
import jax.numpy as jnp
from jax import lax
from jax.experimental import pallas as pl
from jax.experimental.pallas import tpu as pltpu
from jax.sharding import PartitionSpec as P

PG = 4
MESH = pl.DeviceIdType.MESH
F32 = jnp.float32
BF16 = jnp.bfloat16


def column_of(row):
    n = row.shape[1]
    eye = lax.broadcasted_iota(jnp.int32, (n, n), 0) == lax.broadcasted_iota(jnp.int32, (n, n), 1)
    return jnp.sum(jnp.where(eye, jnp.broadcast_to(row, (n, n)), F32(0.0)), axis=1, keepdims=True)


def group_terms(g, basis, res_ref, sig_ref, cnt_ref, pul_ref, ecorr_ref):
    slots, rows, width = basis.shape
    sig = sig_ref[g].astype(F32)
    res = res_ref[g].astype(F32)
    counts = column_of(cnt_ref[pl.ds(g, 1), :].astype(F32))
    pulsar = column_of(pul_ref[pl.ds(g, 1), :].astype(F32))
    lane = lax.broadcasted_iota(jnp.int32, (slots, rows), 1)
    valid = lane.astype(F32) < counts
    var = sig * sig
    inverse = jnp.where(valid, 1.0 / var, F32(0.0))
    total = jnp.sum(inverse, axis=1, keepdims=True)
    n_table = ecorr_ref.shape[1]
    table = lax.broadcasted_iota(jnp.int32, (slots, n_table), 1).astype(F32)
    ids = pulsar + (g * PG).astype(F32)
    chosen = jnp.sum(
        jnp.where(ids == table, jnp.broadcast_to(ecorr_ref[...], (slots, n_table)), F32(0.0)),
        axis=1,
        keepdims=True,
    )
    jitter = chosen * chosen
    coef = jitter / (1.0 + jitter * total)
    wsum = jnp.sum(inverse * res, axis=1, keepdims=True)
    first = lane == 0
    chi = inverse * res * res - jnp.where(first, coef * wsum * wsum, F32(0.0))
    logdet = jnp.where(valid, jnp.log(var), F32(0.0)) + jnp.where(
        first, jnp.log(1.0 + jitter * total), F32(0.0)
    )
    tot = jnp.concatenate(
        [jnp.sum(logdet, axis=0, keepdims=True), jnp.sum(chi, axis=0, keepdims=True)], axis=1
    )

    inv_t = inverse.T
    adj_t = (coef * inverse).T
    blocks = [basis[s] for s in range(slots)]
    weighted = [
        (inv_t[:, s : s + 1] * blocks[s].astype(F32)).astype(BF16) for s in range(slots)
    ]
    member = lax.broadcasted_iota(jnp.int32, (PG, rows), 0).astype(F32)
    onehot = jnp.concatenate(
        [
            jnp.where(member == jnp.broadcast_to(pulsar[s : s + 1], (PG, rows)), F32(1.0), F32(0.0))
            for s in range(slots)
        ],
        axis=1,
    )
    slot = lax.broadcasted_iota(jnp.int32, (slots, rows), 0)
    marks = jnp.concatenate(
        [jnp.where(slot == s, F32(1.0), F32(0.0)) for s in range(slots)], axis=1
    )
    res_row = jnp.concatenate([res[s : s + 1] for s in range(slots)], axis=1)
    left = jnp.concatenate([marks, onehot * res_row, onehot], axis=0).astype(BF16)
    sums = jnp.dot(left, jnp.concatenate(weighted, axis=0), preferred_element_type=F32)
    column = sums[:slots]
    project = sums[slots : slots + PG]
    cw = coef * wsum
    minus = jnp.concatenate(
        [
            jnp.sum(jnp.where(pulsar == F32(m), cw, F32(0.0)) * column, axis=0, keepdims=True)
            for m in range(PG)
        ],
        axis=0,
    )
    rhs = project - minus
    adjusted = jnp.concatenate(
        [
            (weighted[s].astype(F32) - adj_t[:, s : s + 1] * column[s : s + 1]).astype(BF16)
            for s in range(slots)
        ],
        axis=0,
    )
    turned = jnp.concatenate([b.T for b in blocks], axis=1)
    pick = onehot.astype(BF16)

    def gram(m):
        return jnp.dot(turned * pick[m : m + 1], adjusted, preferred_element_type=F32)

    return gram, rhs, tot


def triangle(n):
    return lax.broadcasted_iota(jnp.int32, (n, n), 0), lax.broadcasted_iota(jnp.int32, (n, n), 1)


def pack(full):
    hw = full.shape[0] // 2
    r, c = triangle(hw)
    low = full[hw:, hw:]
    diag = jnp.sum(jnp.where(r == c, low, F32(0.0)), axis=0, keepdims=True)
    both = jnp.where(r <= c, full[:hw, :hw], low)
    return jnp.concatenate([full[:hw, hw:], both, jnp.broadcast_to(diag, (16, hw))], axis=0)


def unpack(packed):
    hw = packed.shape[1]
    r, c = triangle(hw)
    cross, both = packed[:hw], packed[hw : 2 * hw]
    diag = jnp.broadcast_to(packed[2 * hw : 2 * hw + 1], (hw, hw))
    turned = both.T
    top = jnp.concatenate([jnp.where(r <= c, both, turned), cross], axis=1)
    low = jnp.where(r > c, both, jnp.where(r == c, diag, turned))
    return jnp.concatenate([top, jnp.concatenate([cross.T, low], axis=1)], axis=0)


def kernel(
    ndp,
    basis_ref, res_in, sig_in, cnt_in, pul_in, ecorr_in,
    gram_ref, rhs_ref, tot_ref,
    bbuf, res_ref, sig_ref, cnt_ref, pul_ref, ecorr_ref, out_c, in_c, out_y, in_y, whole, out_x, in_x, out_z, in_z,
    s_core, r_core, s_y, r_y, s_x, r_x, s_z, r_z,
    load_sem, send_sem, recv_sem,
):
    nz = ndp // 2
    dp = lax.axis_index("dp")
    psr = lax.axis_index("psr")
    c, y = psr % 2, psr // 2
    x, z = dp % 2, dp // 2
    c2, y2, x2 = 1 - c, 1 - y, 1 - x
    core_peer = (dp, y * 2 + c2)
    y_peer = (dp, y2 * 2 + c)
    x_peer = (z * 2 + x2, psr)
    order = (y2 * 2 + c2, y2 * 2 + c, y * 2 + c2, psr)

    small_loads = []
    pairs = ((sig_in, sig_ref), (cnt_in, cnt_ref), (res_in, res_ref), (pul_in, pul_ref))
    for i, (src, dst) in enumerate(pairs + ((ecorr_in, ecorr_ref),)):
        load = pltpu.make_async_copy(src, dst, load_sem.at[len(order) + i])
        load.start()
        small_loads.append(load)
    loads = []
    for i, g in enumerate(order):
        load = pltpu.make_async_copy(basis_ref.at[g], bbuf.at[i], load_sem.at[i])
        load.start()
        loads.append(load)

    z_peers = [(((z + k) % nz) * 2 + x, psr) for k in range(1, nz)]
    barrier = pltpu.get_barrier_semaphore()
    for peer in [core_peer, y_peer, x_peer] + z_peers:
        pl.semaphore_signal(barrier, inc=1, device_id=peer, device_id_type=MESH)

    copies = []

    def send(src, dst, peer):
        i = len(copies)
        copy = pltpu.make_async_remote_copy(
            src_ref=src, dst_ref=dst, send_sem=send_sem.at[i], recv_sem=recv_sem.at[i],
            device_id=peer, device_id_type=MESH,
        )
        copy.start()
        copies.append(copy)
        return copy

    def terms(i):
        loads[i].wait()
        return group_terms(order[i], bbuf.at[i], res_ref, sig_ref, cnt_ref, pul_ref, ecorr_ref)

    def core_send(n, value):
        out_c[n] = value.astype(BF16)
        return send(out_c.at[n], in_c.at[n], core_peer)

    for load in small_loads:
        load.wait()
    gram0, rhs0, tot = terms(0)
    first = pack(gram0(0))
    pl.semaphore_wait(barrier, 2 + nz)
    core = [core_send(0, first), core_send(1, pack(gram0(1)))]
    gram1, rhs1, t = terms(1)
    tot = tot + t
    y_copies = []
    for m in range(PG):
        own = pack(gram1(m))
        core[m].wait_recv()
        out_y[m] = (own + in_c[m].astype(F32)).astype(BF16)
        y_copies.append(send(out_y.at[m], in_y.at[m], y_peer))
        if m + 2 < PG:
            core.append(core_send(m + 2, pack(gram0(m + 2))))

    gram2, rhs2, t = terms(2)
    tot = tot + t
    for m in range(PG):
        core.append(core_send(PG + m, pack(gram2(m))))
    gram3, rhs3, t = terms(3)
    tot = tot + t
    pad = jnp.zeros((3, tot.shape[1]), F32)
    s_core[...] = jnp.concatenate([rhs0, rhs2, tot, pad, jnp.zeros((4, tot.shape[1]), F32)], axis=0)
    small_c = send(s_core, r_core, core_peer)

    x_copies = []
    z_copies = []

    def to_x(m):
        own = pack(gram3(m))
        core[PG + m].wait_recv()
        own = own + in_c[PG + m].astype(F32)
        y_copies[m].wait_recv()
        full = unpack(own + in_y[m].astype(F32)).reshape(whole.shape[1:])
        whole[m] = full
        out_x[m] = full.astype(BF16)
        x_copies.append(send(out_x.at[m, :, x2], in_x.at[m], x_peer))

    def to_z(m):
        x_copies[m].wait_recv()
        sent = []
        for k in range(1, nz):
            zt = (z + k) % nz
            out_z[m, k - 1] = (whole[m, zt, x] + in_x[m, zt].astype(F32)).astype(BF16)
            sent.append(send(out_z.at[m, k - 1], in_z.at[m, k - 1], z_peers[k - 1]))
        z_copies.append(sent)

    to_x(0)
    small_c.wait_recv()
    rhs1 = rhs1 + r_core[0:PG]
    rhs3 = rhs3 + r_core[PG : 2 * PG]
    tot = tot + r_core[2 * PG : 2 * PG + 1]
    s_y[...] = jnp.concatenate([rhs1, tot, pad], axis=0)
    small_y = send(s_y, r_y, y_peer)
    to_x(1)
    to_z(0)
    to_x(2)
    to_z(1)
    small_y.wait_recv()
    rhs3 = rhs3 + r_y[0:PG]
    tot = tot + r_y[PG : PG + 1]
    s_x[...] = jnp.concatenate([rhs3, tot, pad], axis=0)
    small_x = send(s_x, r_x, x_peer)
    for m in range(3, PG):
        to_x(m)
        to_z(m - 1)
    small_x.wait_recv()
    rhs3 = rhs3 + r_x[0:PG]
    tot = tot + r_x[PG : PG + 1]
    s_z[...] = jnp.concatenate([rhs3, tot, pad], axis=0)
    small_z = [send(s_z, r_z.at[k - 1], z_peers[k - 1]) for k in range(1, nz)]
    to_z(PG - 1)

    def finish(m):
        acc = whole[m, z, x] + in_x[m, z].astype(F32)
        for k in range(1, nz):
            z_copies[m][k - 1].wait_recv()
            acc = acc + in_z[m, k - 1].astype(F32)
        gram_ref[m] = acc

    for m in range(PG - 1):
        finish(m)
    for k in range(1, nz):
        small_z[k - 1].wait_recv()
        rhs3 = rhs3 + r_z[k - 1, 0:PG]
        tot = tot + r_z[k - 1, PG : PG + 1]
    share = rhs_ref.shape[1]
    mine = jnp.zeros((PG, share), F32)
    for e in range(ndp):
        mine = mine + jnp.where(dp == e, rhs3[:, e * share : (e + 1) * share], F32(0.0))
    rhs_ref[...] = mine
    tot_ref[...] = tot
    finish(PG - 1)
    for copy in copies:
        copy.wait_send()


def scale_kernel(norm_rows, all_rows, gram_in, rhs_in, tot_in, gram_ref, rhs_ref, tot_ref):
    gram_ref[...] = gram_in[...] / norm_rows
    rhs_ref[...] = rhs_in[...] / norm_rows
    rows = tot_in.shape[1] // 2
    tot_ref[0] = jnp.sum(tot_in[:, :rows]) / all_rows
    tot_ref[1] = jnp.sum(tot_in[:, rows:]) / all_rows


def fused(basis, residual, sigma, counts, pulsar, ecorr):
    ndp = lax.axis_size("dp")
    groups, slots, rows, width = basis.shape[1:]
    share = width // ndp
    nz = ndp // 2
    norm_rows = float(ndp * slots * rows)
    all_rows = float(ndp * groups * groups * slots * rows)
    vmem = pl.BlockSpec(memory_space=pltpu.VMEM)
    packed = (width + 16, width // 2)
    n_copies = 4 * PG + (nz - 1) * (PG + 1) + 3
    small = pltpu.VMEM((2 * PG, width), F32)
    sums = pl.pallas_call(
        functools.partial(kernel, ndp),
        out_shape=(
            pltpu.VMEM((PG, share, width), F32),
            pltpu.VMEM((PG, share), F32),
            pltpu.VMEM((1, 2 * rows), F32),
        ),
        in_specs=[pl.BlockSpec(memory_space=pltpu.HBM)] * 6,
        out_specs=(vmem, vmem, vmem),
        scratch_shapes=[
            pltpu.VMEM((groups, slots, rows, width), BF16),
            pltpu.VMEM((groups, slots, rows), BF16),
            pltpu.VMEM((groups, slots, rows), BF16),
            pltpu.VMEM((groups, slots), jnp.int32),
            pltpu.VMEM((groups, slots), jnp.int32),
            pltpu.VMEM((1, ecorr.shape[0]), F32),
            pltpu.VMEM((2 * PG,) + packed, BF16),
            pltpu.VMEM((2 * PG,) + packed, BF16),
            pltpu.VMEM((PG,) + packed, BF16),
            pltpu.VMEM((PG,) + packed, BF16),
            pltpu.VMEM((PG, nz, 2, share, width), F32),
            pltpu.VMEM((PG, nz, 2, share, width), BF16),
            pltpu.VMEM((PG, nz, share, width), BF16),
            pltpu.VMEM((PG, nz - 1, share, width), BF16),
            pltpu.VMEM((PG, nz - 1, share, width), BF16),
            pltpu.VMEM((4 * PG, width), F32),
            pltpu.VMEM((4 * PG, width), F32),
            small, small, small, small, small,
            pltpu.VMEM((nz - 1, 2 * PG, width), F32),
            pltpu.SemaphoreType.DMA((groups + 5,)),
            pltpu.SemaphoreType.DMA((n_copies,)),
            pltpu.SemaphoreType.DMA((n_copies,)),
        ],
        compiler_params=pltpu.CompilerParams(
            collective_id=0, has_side_effects=True
        ),
    )(basis[0], residual[0], sigma[0], counts[0], pulsar[0], ecorr.reshape(1, -1))
    return pl.pallas_call(
        functools.partial(scale_kernel, norm_rows, all_rows),
        out_shape=(
            jax.ShapeDtypeStruct((PG, share, width), F32),
            jax.ShapeDtypeStruct((PG, share), F32),
            jax.ShapeDtypeStruct((2,), F32),
        ),
        in_specs=[vmem] * 3,
        out_specs=(vmem, vmem, pl.BlockSpec(memory_space=pltpu.SMEM)),
    )(*[pltpu.with_memory_space_constraint(a, pltpu.VMEM) for a in sums])


def slot_terms(basis, residual, sigma, counts, pulsar, group_ids, ecorr):
    sig = sigma.astype(jnp.float32)
    res = residual.astype(jnp.float32)
    rowpos = lax.broadcasted_iota(jnp.int32, sig.shape, 2)
    valid = rowpos < counts[..., None]
    inverse = jnp.where(valid, 1.0 / (sig * sig), jnp.float32(0.0))
    weighted = (inverse[..., None] * basis).astype(jnp.bfloat16)
    global_id = group_ids[:, None] * PG + pulsar
    table = jnp.arange(ecorr.shape[0], dtype=jnp.int32)
    chosen = jnp.sum(jnp.where(global_id[..., None] == table, ecorr, jnp.float32(0.0)), axis=-1)
    jitter = chosen * chosen
    total = jnp.sum(inverse, axis=2)
    coef = jitter / (1.0 + jitter * total)
    column = jnp.sum(weighted.astype(jnp.float32), axis=2)
    project = jnp.sum(weighted.astype(jnp.float32) * res[..., None], axis=2)
    wsum = jnp.sum(inverse * res, axis=2)
    chi = jnp.sum(inverse * res * res) - jnp.sum(coef * wsum * wsum)
    logdet = jnp.sum(jnp.where(valid, jnp.log(sig * sig), jnp.float32(0.0))) + jnp.sum(
        jnp.log(1.0 + jitter * total)
    )
    adjusted = project - (coef * wsum)[..., None] * column
    grams = []
    sums = []
    for member in range(PG):
        picked = pulsar == member
        masked = jnp.where(picked[..., None, None], weighted, jnp.zeros((), jnp.bfloat16))
        first = jnp.einsum("gslk,gslm->gkm", basis, masked, preferred_element_type=jnp.float32)
        scale = jnp.where(picked, coef, jnp.float32(0.0))
        minus = jnp.einsum(
            "gs,gsk,gsm->gkm", scale, column, column, precision=lax.Precision.HIGHEST
        )
        grams.append(first - minus)
        sums.append(jnp.sum(jnp.where(picked[..., None], adjusted, jnp.float32(0.0)), axis=1))
    return (jnp.stack(grams, axis=1), jnp.stack(sums, axis=1), logdet, chi)


def on_device(basis, residual, sigma, counts, pulsar, ecorr):
    groups = lax.axis_size("psr")
    ndp = lax.axis_size("dp")
    width = basis.shape[-1]
    rows = basis.shape[-2]
    slots = basis.shape[2]
    share = width // ndp
    group_ids = jnp.arange(groups, dtype=jnp.int32)
    gram, rhs, logdet, chi = slot_terms(
        basis[0], residual[0], sigma[0], counts[0], pulsar[0], group_ids, ecorr
    )
    gram_rows = (
        gram.reshape(groups, PG, ndp, share, width)
        .transpose(2, 0, 1, 3, 4)
        .reshape(ndp * groups * PG * share, width)
    )
    rhs_rows = (
        rhs.reshape(groups, PG, ndp, share).transpose(2, 0, 1, 3).reshape(ndp * groups * PG * share)
    )
    gram_part, rhs_part = (
        lax.psum_scatter(gram_rows, ("dp", "psr"), scatter_dimension=0, tiled=True),
        lax.psum_scatter(rhs_rows, ("dp", "psr"), scatter_dimension=0, tiled=True),
    )
    gram_part = gram_part.reshape(PG, share, width)
    rhs_part = rhs_part.reshape(PG, share)
    summed = lax.psum((logdet, chi), ("dp", "psr"))
    norm_rows = float(ndp * slots * rows)
    all_rows = float(ndp * groups * groups * slots * rows)
    totals = jnp.stack([summed[0], summed[1]]) / all_rows
    return (gram_part / norm_rows, rhs_part / norm_rows, totals)


def solution(mesh):
    def step(basis, *rest):
        groups, _, rows, width = basis.shape[1:]
        ndp = lax.axis_size("dp")
        tiled = ndp % 2 == 0 and ndp > 2 and width % (16 * ndp) == 0 and width % 256 == 0 and width == 2 * rows
        if groups == lax.axis_size("psr") == 2 * 2 and tiled:
            return fused(basis, *rest)
        return on_device(basis, *rest)

    return jax.shard_map(
        step,
        mesh=mesh,
        in_specs=(
            P(("dp", "psr"), None, None, None, None),
            P(("dp", "psr"), None, None, None),
            P(("dp", "psr"), None, None, None),
            P(("dp", "psr"), None, None),
            P(("dp", "psr"), None, None),
            P(),
        ),
        out_specs=(P("psr", "dp", None), P("psr", "dp"), P()),
        check_vma=False,
    )
```

```python
import functools

import jax
import jax.numpy as jnp
from jax import lax
from jax.experimental import pallas as pl
from jax.experimental.pallas import tpu as pltpu
from jax.sharding import PartitionSpec as P

PG = 4
MESH = pl.DeviceIdType.MESH
F32 = jnp.float32
BF16 = jnp.bfloat16


def stack_rows(ref, order):
    return jnp.concatenate([ref[g].astype(F32) for g in order], axis=0)


def columns(ref, order, slots):
    rows = [jnp.broadcast_to(ref[pl.ds(g, 1), :].astype(F32), (slots, slots)) for g in order]
    eye = jnp.concatenate([jnp.where(r == c, F32(1.0), F32(0.0)) for r, c in [triangle(slots)]] * len(order), axis=0)
    return jnp.sum(jnp.concatenate(rows, axis=0) * eye, axis=1, keepdims=True)


def slot_weights(order, res_ref, sig_ref, cnt_ref, pul_ref, ecorr_ref):
    slots, rows = sig_ref.shape[1:]
    n = len(order) * slots
    sig = stack_rows(sig_ref, order)
    res = stack_rows(res_ref, order)
    counts = columns(cnt_ref, order, slots)
    pulsar = columns(pul_ref, order, slots)
    base = jnp.concatenate([jnp.full((slots, 1), (g * PG).astype(F32)) for g in order], axis=0)
    lane = lax.broadcasted_iota(jnp.int32, (n, rows), 1)
    valid = lane.astype(F32) < counts
    var = sig * sig
    inverse = jnp.where(valid, 1.0 / var, F32(0.0))
    total = jnp.sum(inverse, axis=1, keepdims=True)
    n_table = ecorr_ref.shape[1]
    table = lax.broadcasted_iota(jnp.int32, (n, n_table), 1).astype(F32)
    chosen = jnp.sum(
        jnp.where(pulsar + base == table, jnp.broadcast_to(ecorr_ref[...], (n, n_table)), F32(0.0)),
        axis=1,
        keepdims=True,
    )
    jitter = chosen * chosen
    coef = jitter / (1.0 + jitter * total)
    wres = inverse * res
    wsum = jnp.sum(wres, axis=1, keepdims=True)
    first = lane == 0
    chi = wres * res - jnp.where(first, coef * wsum * wsum, F32(0.0))
    logdet = jnp.where(valid, jnp.log(var), F32(0.0)) + jnp.where(
        first, jnp.log(1.0 + jitter * total), F32(0.0)
    )
    tot = jnp.concatenate(
        [jnp.sum(logdet, axis=0, keepdims=True), jnp.sum(chi, axis=0, keepdims=True)], axis=1
    )
    return inverse, wres, coef, coef * wsum, pulsar, tot


def split(value):
    high = value.astype(BF16).astype(F32)
    return high, value - high


def group_left(inverse, wres, pulsar):
    slots, rows = inverse.shape
    slot = lax.broadcasted_iota(jnp.int32, (slots, rows), 0)
    member = lax.broadcasted_iota(jnp.int32, (PG, rows), 0).astype(F32)
    hots = [
        jnp.where(member == jnp.broadcast_to(pulsar[s : s + 1], (PG, rows)), F32(1.0), F32(0.0))
        for s in range(slots)
    ]

    def spread(a):
        return jnp.concatenate([jnp.where(slot == s, a, F32(0.0)) for s in range(slots)], axis=1)

    def hot(a):
        return jnp.concatenate([hots[s] * a[s : s + 1] for s in range(slots)], axis=1)

    left = [spread(a) for a in split(inverse)] + [hot(a) for a in split(wres)]
    return jnp.concatenate(left, axis=0).astype(BF16), hots


def group_terms(basis, left, hots, inverse, coef, cw, pulsar, part, emit):
    slots, rows, width = basis.shape
    hw = width // 2
    sums = jnp.dot(left, basis[...].reshape(slots * rows, width), preferred_element_type=F32)
    column = sums[:slots] + sums[slots : 2 * slots]
    project = sums[2 * slots : 2 * slots + PG] + sums[2 * slots + PG : 2 * slots + 2 * PG]
    minus = jnp.concatenate(
        [
            jnp.sum(jnp.where(pulsar == F32(m), cw, F32(0.0)) * column, axis=0, keepdims=True)
            for m in range(PG)
        ],
        axis=0,
    )
    shift = coef * column
    r, c = triangle(hw)
    for s in range(slots):
        centred = (basis[s].astype(F32) - shift[s : s + 1]).astype(BF16)
        weighted = (basis[s].T.astype(F32) * inverse[s : s + 1]).astype(BF16)
        full = jnp.dot(weighted, centred, preferred_element_type=F32)
        low = full[hw:, hw:]
        part[s, 0:hw] = full[:hw, hw:]
        part[s, hw:width] = jnp.where(r <= c, full[:hw, :hw], low)
        diag = jnp.sum(jnp.where(r == c, low, F32(0.0)), axis=0, keepdims=True)
        part[s, width : width + 16] = jnp.broadcast_to(diag, (16, hw))
    for k in range(0, width + 16, 16):
        pieces = [part[s, k : k + 16] for s in range(slots)]
        for m in range(PG):
            emit(m, k, sum(hots[s][m : m + 1] * pieces[s] for s in range(slots)))
    return project - minus


def triangle(n):
    return lax.broadcasted_iota(jnp.int32, (n, n), 0), lax.broadcasted_iota(jnp.int32, (n, n), 1)


def unpack(packed):
    hw = packed.shape[1]
    r, c = triangle(hw)
    cross = packed[:hw].astype(BF16)
    both = packed[hw : 2 * hw].astype(BF16)
    diag = jnp.broadcast_to(packed[2 * hw : 2 * hw + 1], (hw, hw))
    turned = both.T.astype(F32)
    both = both.astype(F32)
    top = jnp.concatenate([jnp.where(r <= c, both, turned).astype(BF16), cross], axis=1)
    low = jnp.where(r > c, both, jnp.where(r == c, diag, turned)).astype(BF16)
    return jnp.concatenate([top, jnp.concatenate([cross.T, low], axis=1)], axis=0)


def kernel(
    ndp,
    basis_ref, res_in, sig_in, cnt_in, pul_in, ecorr_in,
    gram_ref, rhs_ref, tot_ref,
    buf0, buf1, buf2, buf3, res_ref, sig_ref, cnt_ref, pul_ref, ecorr_ref, part, kept,
    out_c, in_c, out_y, in_y, out_x, in_x, out_z, in_z,
    s_core, r_core, s_y, r_y, s_x, r_x, s_z, r_z,
    load_sem, send_sem, recv_sem,
):
    nz = ndp // 2
    dp = lax.axis_index("dp")
    psr = lax.axis_index("psr")
    c, y = psr % 2, psr // 2
    x, z = dp % 2, dp // 2
    c2, y2, x2 = 1 - c, 1 - y, 1 - x
    core_peer = (dp, y * 2 + c2)
    y_peer = (dp, y2 * 2 + c)
    x_peer = (z * 2 + x2, psr)
    z_peers = [(((z + k) % nz) * 2 + x, psr) for k in range(1, nz)]
    order = (y2 * 2 + c2, y2 * 2 + c, y * 2 + c2, psr)
    bufs = (buf0, buf1, buf2, buf3)

    barrier = pltpu.get_barrier_semaphore()
    for peer in [core_peer, y_peer, x_peer] + z_peers:
        pl.semaphore_signal(barrier, inc=1, device_id=peer, device_id_type=MESH)
    small_loads = []
    pairs = ((sig_in, sig_ref), (cnt_in, cnt_ref), (res_in, res_ref), (pul_in, pul_ref))
    for i, (src, dst) in enumerate(pairs + ((ecorr_in, ecorr_ref),)):
        load = pltpu.make_async_copy(src, dst, load_sem.at[len(order) + i])
        load.start()
        small_loads.append(load)
    loads = []
    for i, g in enumerate(order):
        load = pltpu.make_async_copy(basis_ref.at[g], bufs[i], load_sem.at[i])
        load.start()
        loads.append(load)

    copies = []

    def send(src, dst, peer):
        i = len(copies)
        copy = pltpu.make_async_remote_copy(
            src_ref=src, dst_ref=dst, send_sem=send_sem.at[i], recv_sem=recv_sem.at[i],
            device_id=peer, device_id_type=MESH,
        )
        copy.start()
        copies.append(copy)
        return copy

    for load in small_loads:
        load.wait()
    slots = sig_ref.shape[1]
    inverse, wres, coef, cw, pulsar, tot = slot_weights(order, res_ref, sig_ref, cnt_ref, pul_ref, ecorr_ref)

    def terms(i, emit):
        mine = slice(i * slots, (i + 1) * slots)
        left, hots = group_left(inverse[mine], wres[mine], pulsar[mine])
        loads[i].wait()
        return group_terms(bufs[i], left, hots, inverse[mine], coef[mine], cw[mine], pulsar[mine], part, emit)

    def to_core(base):
        def emit(m, k, value):
            out_c[base + m, k : k + 16] = value.astype(BF16)

        return emit

    def to_kept(base):
        def emit(m, k, value):
            kept[base + m, k : k + 16] = value

        return emit

    with jax.named_scope("terms_a"):
        rhs0 = terms(0, to_core(0))
    with jax.named_scope("barrier"):
        pl.semaphore_wait(barrier, 2 + nz)
    core = [send(out_c.at[m], in_c.at[m], core_peer) for m in range(PG)]
    with jax.named_scope("terms_b"):
        rhs1 = terms(1, to_kept(0))
    y_copies = []
    for m in range(PG):
        with jax.named_scope("core_wait_%d" % m):
            core[m].wait_recv()
        out_y[m] = (kept[m] + in_c[m].astype(F32)).astype(BF16)
        y_copies.append(send(out_y.at[m], in_y.at[m], y_peer))
    with jax.named_scope("terms_c"):
        rhs2 = terms(2, to_core(PG))
    core += [send(out_c.at[PG + m], in_c.at[PG + m], core_peer) for m in range(PG)]
    with jax.named_scope("terms_d"):
        rhs3 = terms(3, to_kept(PG))
    pad = jnp.zeros((3, tot.shape[1]), F32)
    s_core[...] = jnp.concatenate([rhs0, rhs2, tot, pad, jnp.zeros((4, tot.shape[1]), F32)], axis=0)
    small_c = send(s_core, r_core, core_peer)

    x_copies = []
    z_copies = []
    hz = nz // 2

    def to_x(m):
        with jax.named_scope("y_wait_%d" % m):
            core[PG + m].wait_recv()
            y_copies[m].wait_recv()
        own = kept[PG + m] + in_c[PG + m].astype(F32)
        out_x[m] = unpack(own + in_y[m].astype(F32)).reshape(out_x.shape[1:])
        x_copies.append([
            send(out_x.at[m, pl.ds(h * hz, hz), x2], in_x.at[m, pl.ds(h * hz, hz)], x_peer) for h in range(2)
        ])

    def to_z(m):
        with jax.named_scope("x_wait_%d" % m):
            for copy in x_copies[m]:
                copy.wait_recv()
        sent = []
        for k in range(1, nz):
            zt = (z + k) % nz
            out_z[m, k - 1] = (out_x[m, zt, x].astype(F32) + in_x[m, zt].astype(F32)).astype(BF16)
            sent.append(send(out_z.at[m, k - 1], in_z.at[m, k - 1], z_peers[k - 1]))
        z_copies.append(sent)

    to_x(0)
    small_c.wait_recv()
    rhs1 = rhs1 + r_core[0:PG]
    rhs3 = rhs3 + r_core[PG : 2 * PG]
    tot = tot + r_core[2 * PG : 2 * PG + 1]
    s_y[...] = jnp.concatenate([rhs1, tot, pad], axis=0)
    small_y = send(s_y, r_y, y_peer)
    to_x(1)
    to_x(2)
    to_z(0)
    small_y.wait_recv()
    rhs3 = rhs3 + r_y[0:PG]
    tot = tot + r_y[PG : PG + 1]
    s_x[...] = jnp.concatenate([rhs3, tot, pad], axis=0)
    small_x = send(s_x, r_x, x_peer)
    to_x(3)
    to_z(1)
    to_z(2)
    small_x.wait_recv()
    rhs3 = rhs3 + r_x[0:PG]
    tot = tot + r_x[PG : PG + 1]
    s_z[...] = jnp.concatenate([rhs3, tot, pad], axis=0)
    small_z = [send(s_z, r_z.at[k - 1], z_peers[k - 1]) for k in range(1, nz)]
    to_z(3)

    def finish(m):
        acc = out_x[m, z, x].astype(F32) + in_x[m, z].astype(F32)
        with jax.named_scope("z_wait_%d" % m):
            for k in range(1, nz):
                z_copies[m][k - 1].wait_recv()
        for k in range(1, nz):
            acc = acc + in_z[m, k - 1].astype(F32)
        gram_ref[m] = acc

    for m in range(PG - 1):
        finish(m)
    for k in range(1, nz):
        small_z[k - 1].wait_recv()
        rhs3 = rhs3 + r_z[k - 1, 0:PG]
        tot = tot + r_z[k - 1, PG : PG + 1]
    share = rhs_ref.shape[1]
    mine = jnp.zeros((PG, share), F32)
    for e in range(ndp):
        mine = mine + jnp.where(dp == e, rhs3[:, e * share : (e + 1) * share], F32(0.0))
    rhs_ref[...] = mine
    tot_ref[...] = tot
    finish(PG - 1)
    for copy in copies:
        copy.wait_send()


def scale_kernel(norm_rows, all_rows, gram_in, rhs_in, tot_in, gram_ref, rhs_ref, tot_ref):
    gram_ref[...] = gram_in[...] / norm_rows
    rhs_ref[...] = rhs_in[...] / norm_rows
    rows = tot_in.shape[1] // 2
    tot_ref[0] = jnp.sum(tot_in[:, :rows]) / all_rows
    tot_ref[1] = jnp.sum(tot_in[:, rows:]) / all_rows


def fused(basis, residual, sigma, counts, pulsar, ecorr):
    ndp = lax.axis_size("dp")
    groups, slots, rows, width = basis.shape[1:]
    share = width // ndp
    nz = ndp // 2
    norm_rows = float(ndp * slots * rows)
    all_rows = float(ndp * groups * groups * slots * rows)
    vmem = pl.BlockSpec(memory_space=pltpu.VMEM)
    packed = (width + 16, width // 2)
    n_copies = 5 * PG + (nz - 1) * (PG + 1) + 3
    small = pltpu.VMEM((2 * PG, width), F32)
    sums = pl.pallas_call(
        functools.partial(kernel, ndp),
        out_shape=(
            pltpu.VMEM((PG, share, width), F32),
            pltpu.VMEM((PG, share), F32),
            pltpu.VMEM((1, 2 * rows), F32),
        ),
        in_specs=[pl.BlockSpec(memory_space=pltpu.HBM)] * 6,
        out_specs=(vmem, vmem, vmem),
        scratch_shapes=[
            pltpu.VMEM((slots, rows, width), BF16),
            pltpu.VMEM((slots, rows, width), BF16),
            pltpu.VMEM((slots, rows, width), BF16),
            pltpu.VMEM((slots, rows, width), BF16),
            pltpu.VMEM((groups, slots, rows), BF16),
            pltpu.VMEM((groups, slots, rows), BF16),
            pltpu.VMEM((groups, slots), jnp.int32),
            pltpu.VMEM((groups, slots), jnp.int32),
            pltpu.VMEM((1, ecorr.shape[0]), F32),
            pltpu.VMEM((slots,) + packed, F32),
            pltpu.VMEM((2 * PG,) + packed, F32),
            pltpu.VMEM((2 * PG,) + packed, BF16),
            pltpu.VMEM((2 * PG,) + packed, BF16),
            pltpu.VMEM((PG,) + packed, BF16),
            pltpu.VMEM((PG,) + packed, BF16),
            pltpu.VMEM((PG, nz, 2, share, width), BF16),
            pltpu.VMEM((PG, nz, share, width), BF16),
            pltpu.VMEM((PG, nz - 1, share, width), BF16),
            pltpu.VMEM((PG, nz - 1, share, width), BF16),
            pltpu.VMEM((4 * PG, width), F32),
            pltpu.VMEM((4 * PG, width), F32),
            small, small, small, small, small,
            pltpu.VMEM((nz - 1, 2 * PG, width), F32),
            pltpu.SemaphoreType.DMA((groups + 5,)),
            pltpu.SemaphoreType.DMA((n_copies,)),
            pltpu.SemaphoreType.DMA((n_copies,)),
        ],
        compiler_params=pltpu.CompilerParams(
            collective_id=0, has_side_effects=True
        ),
    )(basis[0], residual[0], sigma[0], counts[0], pulsar[0], ecorr.reshape(1, -1))
    return pl.pallas_call(
        functools.partial(scale_kernel, norm_rows, all_rows),
        out_shape=(
            jax.ShapeDtypeStruct((PG, share, width), F32),
            jax.ShapeDtypeStruct((PG, share), F32),
            jax.ShapeDtypeStruct((2,), F32),
        ),
        in_specs=[vmem] * 3,
        out_specs=(vmem, vmem, pl.BlockSpec(memory_space=pltpu.SMEM)),
    )(*[pltpu.with_memory_space_constraint(a, pltpu.VMEM) for a in sums])


def slot_terms(basis, residual, sigma, counts, pulsar, group_ids, ecorr):
    sig = sigma.astype(jnp.float32)
    res = residual.astype(jnp.float32)
    rowpos = lax.broadcasted_iota(jnp.int32, sig.shape, 2)
    valid = rowpos < counts[..., None]
    inverse = jnp.where(valid, 1.0 / (sig * sig), jnp.float32(0.0))
    weighted = (inverse[..., None] * basis).astype(jnp.bfloat16)
    global_id = group_ids[:, None] * PG + pulsar
    table = jnp.arange(ecorr.shape[0], dtype=jnp.int32)
    chosen = jnp.sum(jnp.where(global_id[..., None] == table, ecorr, jnp.float32(0.0)), axis=-1)
    jitter = chosen * chosen
    total = jnp.sum(inverse, axis=2)
    coef = jitter / (1.0 + jitter * total)
    column = jnp.sum(weighted.astype(jnp.float32), axis=2)
    project = jnp.sum(weighted.astype(jnp.float32) * res[..., None], axis=2)
    wsum = jnp.sum(inverse * res, axis=2)
    chi = jnp.sum(inverse * res * res) - jnp.sum(coef * wsum * wsum)
    logdet = jnp.sum(jnp.where(valid, jnp.log(sig * sig), jnp.float32(0.0))) + jnp.sum(
        jnp.log(1.0 + jitter * total)
    )
    adjusted = project - (coef * wsum)[..., None] * column
    grams = []
    sums = []
    for member in range(PG):
        picked = pulsar == member
        masked = jnp.where(picked[..., None, None], weighted, jnp.zeros((), jnp.bfloat16))
        first = jnp.einsum("gslk,gslm->gkm", basis, masked, preferred_element_type=jnp.float32)
        scale = jnp.where(picked, coef, jnp.float32(0.0))
        minus = jnp.einsum(
            "gs,gsk,gsm->gkm", scale, column, column, precision=lax.Precision.HIGHEST
        )
        grams.append(first - minus)
        sums.append(jnp.sum(jnp.where(picked[..., None], adjusted, jnp.float32(0.0)), axis=1))
    return (jnp.stack(grams, axis=1), jnp.stack(sums, axis=1), logdet, chi)


def on_device(basis, residual, sigma, counts, pulsar, ecorr):
    groups = lax.axis_size("psr")
    ndp = lax.axis_size("dp")
    width = basis.shape[-1]
    rows = basis.shape[-2]
    slots = basis.shape[2]
    share = width // ndp
    group_ids = jnp.arange(groups, dtype=jnp.int32)
    gram, rhs, logdet, chi = slot_terms(
        basis[0], residual[0], sigma[0], counts[0], pulsar[0], group_ids, ecorr
    )
    gram_rows = (
        gram.reshape(groups, PG, ndp, share, width)
        .transpose(2, 0, 1, 3, 4)
        .reshape(ndp * groups * PG * share, width)
    )
    rhs_rows = (
        rhs.reshape(groups, PG, ndp, share).transpose(2, 0, 1, 3).reshape(ndp * groups * PG * share)
    )
    gram_part, rhs_part = (
        lax.psum_scatter(gram_rows, ("dp", "psr"), scatter_dimension=0, tiled=True),
        lax.psum_scatter(rhs_rows, ("dp", "psr"), scatter_dimension=0, tiled=True),
    )
    gram_part = gram_part.reshape(PG, share, width)
    rhs_part = rhs_part.reshape(PG, share)
    summed = lax.psum((logdet, chi), ("dp", "psr"))
    norm_rows = float(ndp * slots * rows)
    all_rows = float(ndp * groups * groups * slots * rows)
    totals = jnp.stack([summed[0], summed[1]]) / all_rows
    return (gram_part / norm_rows, rhs_part / norm_rows, totals)


def solution(mesh):
    def step(basis, *rest):
        groups, _, rows, width = basis.shape[1:]
        ndp = lax.axis_size("dp")
        tiled = ndp % 4 == 0 and width % (16 * ndp) == 0 and width % 256 == 0 and width == 2 * rows
        if groups == lax.axis_size("psr") == 2 * 2 and tiled:
            return fused(basis, *rest)
        return on_device(basis, *rest)

    return jax.shard_map(
        step,
        mesh=mesh,
        in_specs=(
            P(("dp", "psr"), None, None, None, None),
            P(("dp", "psr"), None, None, None),
            P(("dp", "psr"), None, None, None),
            P(("dp", "psr"), None, None),
            P(("dp", "psr"), None, None),
            P(),
        ),
        out_specs=(P("psr", "dp", None), P("psr", "dp"), P()),
        check_vma=False,
    )
```

```python
import functools

import jax
import jax.numpy as jnp
from jax import lax
from jax.experimental import pallas as pl
from jax.experimental.pallas import tpu as pltpu
from jax.sharding import PartitionSpec as P

PG = 4
MESH = pl.DeviceIdType.MESH
F32 = jnp.float32
BF16 = jnp.bfloat16


def stack_rows(ref, order):
    return jnp.concatenate([ref[g].astype(F32) for g in order], axis=0)


def columns(ref, order, slots):
    rows = [jnp.broadcast_to(ref[pl.ds(g, 1), :].astype(F32), (slots, slots)) for g in order]
    eye = jnp.concatenate([jnp.where(r == c, F32(1.0), F32(0.0)) for r, c in [triangle(slots)]] * len(order), axis=0)
    return jnp.sum(jnp.concatenate(rows, axis=0) * eye, axis=1, keepdims=True)


def slot_weights(order, res_ref, sig_ref, cnt_ref, pul_ref, ecorr_ref):
    slots, rows = sig_ref.shape[1:]
    n = len(order) * slots
    sig = stack_rows(sig_ref, order)
    res = stack_rows(res_ref, order)
    counts = columns(cnt_ref, order, slots)
    pulsar = columns(pul_ref, order, slots)
    base = jnp.concatenate([jnp.full((slots, 1), (g * PG).astype(F32)) for g in order], axis=0)
    lane = lax.broadcasted_iota(jnp.int32, (n, rows), 1)
    valid = lane.astype(F32) < counts
    var = sig * sig
    inverse = jnp.where(valid, 1.0 / var, F32(0.0))
    total = jnp.sum(inverse, axis=1, keepdims=True)
    n_table = ecorr_ref.shape[1]
    table = lax.broadcasted_iota(jnp.int32, (n, n_table), 1).astype(F32)
    chosen = jnp.sum(
        jnp.where(pulsar + base == table, jnp.broadcast_to(ecorr_ref[...], (n, n_table)), F32(0.0)),
        axis=1,
        keepdims=True,
    )
    jitter = chosen * chosen
    coef = jitter / (1.0 + jitter * total)
    wres = inverse * res
    wsum = jnp.sum(wres, axis=1, keepdims=True)
    first = lane == 0
    chi = wres * res - jnp.where(first, coef * wsum * wsum, F32(0.0))
    logdet = jnp.where(valid, jnp.log(var), F32(0.0)) + jnp.where(
        first, jnp.log(1.0 + jitter * total), F32(0.0)
    )
    tot = jnp.concatenate(
        [jnp.sum(logdet, axis=0, keepdims=True), jnp.sum(chi, axis=0, keepdims=True)], axis=1
    )
    return inverse, wres, coef, coef * wsum, pulsar, tot


def split(value):
    high = value.astype(BF16).astype(F32)
    return high, value - high


def group_left(inverse, wres, pulsar):
    slots, rows = inverse.shape
    slot = lax.broadcasted_iota(jnp.int32, (slots, rows), 0)
    member = lax.broadcasted_iota(jnp.int32, (PG, rows), 0).astype(F32)
    hots = [
        jnp.where(member == jnp.broadcast_to(pulsar[s : s + 1], (PG, rows)), F32(1.0), F32(0.0))
        for s in range(slots)
    ]

    def spread(a):
        return jnp.concatenate([jnp.where(slot == s, a, F32(0.0)) for s in range(slots)], axis=1)

    def hot(a):
        return jnp.concatenate([hots[s] * a[s : s + 1] for s in range(slots)], axis=1)

    left = [spread(a) for a in split(inverse)] + [hot(a) for a in split(wres)]
    return jnp.concatenate(left, axis=0).astype(BF16), hots


def group_terms(basis, left, hots, inverse, coef, cw, pulsar, part, emit):
    slots, rows, width = basis.shape
    hw = width // 2
    sums = jnp.dot(left, basis[...].reshape(slots * rows, width), preferred_element_type=F32)
    column = sums[:slots] + sums[slots : 2 * slots]
    project = sums[2 * slots : 2 * slots + PG] + sums[2 * slots + PG : 2 * slots + 2 * PG]
    minus = jnp.concatenate(
        [
            jnp.sum(jnp.where(pulsar == F32(m), cw, F32(0.0)) * column, axis=0, keepdims=True)
            for m in range(PG)
        ],
        axis=0,
    )
    shift = coef * column
    r, c = triangle(hw)
    ends = []
    for s in range(slots):
        centred = (basis[s].astype(F32) - shift[s : s + 1]).astype(BF16)
        weighted = (basis[s].T.astype(F32) * inverse[s : s + 1]).astype(BF16)
        full = jnp.dot(weighted, centred, preferred_element_type=F32)
        low = full[hw:, hw:]
        part[s, 0] = full[:hw, hw:]
        part[s, 1] = jnp.where(r <= c, full[:hw, :hw], low)
        ends.append(jnp.sum(jnp.where(r == c, low, F32(0.0)), axis=0, keepdims=True))
    for h in range(2):
        for k in range(0, hw, 16):
            pieces = [part[s, h, k : k + 16] for s in range(slots)]
            for m in range(PG):
                emit(m, h, k, sum(hots[s][m : m + 1] * pieces[s] for s in range(slots)))
    ends = jnp.concatenate(ends, axis=0)
    diag = [
        jnp.sum(jnp.where(pulsar == F32(m), ends, F32(0.0)), axis=0, keepdims=True) for m in range(PG)
    ]
    return project - minus, diag


def triangle(n):
    return lax.broadcasted_iota(jnp.int32, (n, n), 0), lax.broadcasted_iota(jnp.int32, (n, n), 1)


def small_tiles(ref, rhs, diag, tot):
    hw = rhs.shape[1] // 2
    for h in range(2):
        rows = [rhs[:, h * hw : (h + 1) * hw], tot[:, :hw], tot[:, hw:]] + diag[h * PG // 2 : (h + 1) * PG // 2]
        ref[h] = jnp.concatenate(rows, axis=0)


def kernel(
    ndp,
    basis_ref, res_in, sig_in, cnt_in, pul_in, ecorr_in,
    gram_ref, rhs_ref, tot_ref,
    buf0, buf1, buf2, buf3, res_ref, sig_ref, cnt_ref, pul_ref, ecorr_ref, part, kept,
    out_c, in_c, out_f, out_n, in_p, out_d, in_d,
    s_core, r_core, s_near, s_far, r_p, s_z, r_z,
    load_sem, send_sem, recv_sem,
):
    nz = ndp // 2
    dp = lax.axis_index("dp")
    psr = lax.axis_index("psr")
    c, y = psr % 2, psr // 2
    x, z = dp % 2, dp // 2
    c2, y2, x2 = 1 - c, 1 - y, 1 - x
    core_peer = (dp, y * 2 + c2)
    y_peer = (dp, y2 * 2 + c)
    x_peer = (z * 2 + x2, psr)
    xy_peer = (z * 2 + x2, y2 * 2 + c)
    steps = [(k, j) for k in range(1, nz) for j in range(2)] + [(0, 1)]
    dp_peers = {(k, j): (((z + k) % nz) * 2 + (x + j) % 2, psr) for k, j in steps}
    order = (y2 * 2 + c2, y2 * 2 + c, y * 2 + c2, psr)
    bufs = (buf0, buf1, buf2, buf3)

    barrier = pltpu.get_barrier_semaphore()
    greeted = [core_peer, y_peer, xy_peer] + list(dp_peers.values())
    for peer in greeted:
        pl.semaphore_signal(barrier, inc=1, device_id=peer, device_id_type=MESH)
    small_loads = []
    pairs = ((sig_in, sig_ref), (cnt_in, cnt_ref), (res_in, res_ref), (pul_in, pul_ref))
    for i, (src, dst) in enumerate(pairs + ((ecorr_in, ecorr_ref),)):
        load = pltpu.make_async_copy(src, dst, load_sem.at[len(order) + i])
        load.start()
        small_loads.append(load)
    loads = []
    for i, g in enumerate(order):
        load = pltpu.make_async_copy(basis_ref.at[g], bufs[i], load_sem.at[i])
        load.start()
        loads.append(load)

    copies = []

    def send(src, dst, peer):
        i = len(copies)
        copy = pltpu.make_async_remote_copy(
            src_ref=src, dst_ref=dst, send_sem=send_sem.at[i], recv_sem=recv_sem.at[i],
            device_id=peer, device_id_type=MESH,
        )
        copy.start()
        copies.append(copy)
        return copy

    for load in small_loads:
        load.wait()
    slots = sig_ref.shape[1]
    inverse, wres, coef, cw, pulsar, tot = slot_weights(order, res_ref, sig_ref, cnt_ref, pul_ref, ecorr_ref)

    def terms(i, emit):
        mine = slice(i * slots, (i + 1) * slots)
        left, hots = group_left(inverse[mine], wres[mine], pulsar[mine])
        loads[i].wait()
        return group_terms(bufs[i], left, hots, inverse[mine], coef[mine], cw[mine], pulsar[mine], part, emit)

    def to_core(base):
        def emit(m, h, k, value):
            out_c[base + m, h, k : k + 16] = value.astype(BF16)

        return emit

    def to_kept(base):
        def emit(m, h, k, value):
            kept[base + m, h, k : k + 16] = value

        return emit

    def core_sends(n):
        small = send(s_core.at[n], r_core.at[n], core_peer)
        return [send(out_c.at[n * PG + m], in_c.at[n * PG + m], core_peer) for m in range(PG)], small

    small_tiles(s_core.at[0], *terms(0, to_core(0)), tot)
    pl.semaphore_wait(barrier, len(greeted))
    core_far, small_far = core_sends(0)
    small_tiles(s_far, *terms(1, to_kept(0)), tot)
    small_far.wait_recv()
    s_far[...] = s_far[...] + r_core[0]
    small_p = [send(s_far, r_p.at[0], y_peer), send(s_far, r_p.at[1], xy_peer)]
    plane = [[None] * 3 for _ in range(PG)]

    def far_sum(m):
        core_far[m].wait_recv()
        out_f[m] = (kept[m] + in_c[m].astype(F32)).astype(BF16)

    def to_y(m):
        plane[m][0] = send(out_f.at[m, x], in_p.at[m, 0], y_peer)

    def to_xy(m):
        plane[m][1] = send(out_f.at[m, x2], in_p.at[m, 1], xy_peer)

    def to_x(m):
        core_near[m].wait_recv()
        out_n[m] = (kept[PG + m, x2] + in_c[PG + m, x2].astype(F32)).astype(BF16)
        plane[m][2] = send(out_n.at[m], in_p.at[m, 2], x_peer)

    far_sum(0)
    to_y(0)
    far_sum(1)
    to_y(1)
    to_xy(0)
    far_sum(2)
    to_y(2)
    far_sum(3)
    small_tiles(s_core.at[1], *terms(2, to_core(PG)), tot)
    core_near, small_near = core_sends(1)
    to_y(3)
    to_xy(1)
    small_tiles(s_near, *terms(3, to_kept(PG)), tot)
    small_near.wait_recv()
    s_near[...] = s_near[...] + r_core[1]
    small_p.append(send(s_near, r_p.at[2], x_peer))
    to_x(0)
    to_x(1)
    to_xy(2)
    to_x(2)
    to_xy(3)
    to_x(3)

    total = s_near[...]
    for i in range(3):
        small_p[i].wait_recv()
        total = total + r_p[i]
    s_z[...] = total
    hz = nz // 2
    small_z = [
        send(s_z.at[((z + k) % nz) // hz], r_z.at[k - 1], dp_peers[k, 0]) for k in range(1, nz)
    ]

    hw = out_n.shape[1]
    row, col = triangle(hw)
    crossed = x == 0
    upper = jnp.logical_or(row <= col, crossed)
    lower = jnp.logical_and(row > col, jnp.logical_not(crossed))
    middle = jnp.logical_and(row == col, jnp.logical_not(crossed))
    spread = []

    def to_all(m):
        value = kept[PG + m, x] + in_c[PG + m, x].astype(F32)
        for i in range(3):
            plane[m][i].wait_recv()
            value = value + in_p[m, i].astype(F32)
        value = value.astype(BF16)
        turned = value.T.astype(F32)
        value = value.astype(F32)
        at = PG + 2 + m % (PG // 2)
        diag = jnp.broadcast_to(total[m // (PG // 2), at : at + 1], (hw, hw))
        top = jnp.where(upper, value, turned)
        low = jnp.where(lower, value, jnp.where(middle, diag, turned))
        out_d[m] = jnp.concatenate([top, low], axis=0).astype(BF16).reshape(out_d.shape[1:])
        spread.append({
            (k, j): send(out_d.at[m, (z + k) % nz, (x + j) % 2], in_d.at[m, k, j], dp_peers[k, j])
            for k, j in steps
        })

    def finish(m):
        own = out_d[m, z, x].astype(F32)
        for copy in spread[m].values():
            copy.wait_recv()
        for k in range(1, nz):
            own = own + in_d[m, k, 0].astype(F32)
        other = in_d[m, 0, 1].astype(F32)
        for k in range(1, nz):
            other = other + in_d[m, k, 1].astype(F32)
        swap = (x + z // hz) % 2 == 0
        left = jnp.where(swap, other, own)
        gram_ref[m] = jnp.concatenate([left, jnp.where(swap, own, other)], axis=1)

    for m in range(PG):
        to_all(m)
    for m in range(PG - 1):
        finish(m)
    final = s_z[z // hz]
    for k in range(1, nz):
        small_z[k - 1].wait_recv()
        final = final + r_z[k - 1]
    share = rhs_ref.shape[1]
    mine = jnp.zeros((PG, share), F32)
    for e in range(hw // share):
        mine = mine + jnp.where(dp % (hw // share) == e, final[:PG, e * share : (e + 1) * share], F32(0.0))
    rhs_ref[...] = mine
    tot_ref[...] = jnp.concatenate([final[PG : PG + 1], final[PG + 1 : PG + 2]], axis=1)
    finish(PG - 1)
    for copy in copies:
        copy.wait_send()


def scale_kernel(norm_rows, all_rows, gram_in, rhs_in, tot_in, gram_ref, rhs_ref, tot_ref):
    gram_ref[...] = gram_in[...] / norm_rows
    rhs_ref[...] = rhs_in[...] / norm_rows
    rows = tot_in.shape[1] // 2
    tot_ref[0] = jnp.sum(tot_in[:, :rows]) / all_rows
    tot_ref[1] = jnp.sum(tot_in[:, rows:]) / all_rows


def fused(basis, residual, sigma, counts, pulsar, ecorr):
    ndp = lax.axis_size("dp")
    groups, slots, rows, width = basis.shape[1:]
    share = width // ndp
    nz = ndp // 2
    norm_rows = float(ndp * slots * rows)
    all_rows = float(ndp * groups * groups * slots * rows)
    vmem = pl.BlockSpec(memory_space=pltpu.VMEM)
    hw = width // 2
    tile = (2, 2 * PG, hw)
    n_copies = 2 * (PG + 1) + 3 * (PG + 1) + (ndp - 1) * PG + nz - 1
    sums = pl.pallas_call(
        functools.partial(kernel, ndp),
        out_shape=(
            pltpu.VMEM((PG, share, width), F32),
            pltpu.VMEM((PG, share), F32),
            pltpu.VMEM((1, 2 * rows), F32),
        ),
        in_specs=[pl.BlockSpec(memory_space=pltpu.HBM)] * 6,
        out_specs=(vmem, vmem, vmem),
        scratch_shapes=[
            pltpu.VMEM((slots, rows, width), BF16),
            pltpu.VMEM((slots, rows, width), BF16),
            pltpu.VMEM((slots, rows, width), BF16),
            pltpu.VMEM((slots, rows, width), BF16),
            pltpu.VMEM((groups, slots, rows), BF16),
            pltpu.VMEM((groups, slots, rows), BF16),
            pltpu.VMEM((groups, slots), jnp.int32),
            pltpu.VMEM((groups, slots), jnp.int32),
            pltpu.VMEM((1, ecorr.shape[0]), F32),
            pltpu.VMEM((slots, 2, hw, hw), F32),
            pltpu.VMEM((2 * PG, 2, hw, hw), F32),
            pltpu.VMEM((2 * PG, 2, hw, hw), BF16),
            pltpu.VMEM((2 * PG, 2, hw, hw), BF16),
            pltpu.VMEM((PG, 2, hw, hw), BF16),
            pltpu.VMEM((PG, hw, hw), BF16),
            pltpu.VMEM((PG, 3, hw, hw), BF16),
            pltpu.VMEM((PG, nz, 2, share, hw), BF16),
            pltpu.VMEM((PG, nz, 2, share, hw), BF16),
            pltpu.VMEM((2,) + tile, F32),
            pltpu.VMEM((2,) + tile, F32),
            pltpu.VMEM(tile, F32),
            pltpu.VMEM(tile, F32),
            pltpu.VMEM((3,) + tile, F32),
            pltpu.VMEM(tile, F32),
            pltpu.VMEM((nz - 1,) + tile[1:], F32),
            pltpu.SemaphoreType.DMA((groups + 5,)),
            pltpu.SemaphoreType.DMA((n_copies,)),
            pltpu.SemaphoreType.DMA((n_copies,)),
        ],
        compiler_params=pltpu.CompilerParams(
            collective_id=0, has_side_effects=True
        ),
    )(basis[0], residual[0], sigma[0], counts[0], pulsar[0], ecorr.reshape(1, -1))
    return pl.pallas_call(
        functools.partial(scale_kernel, norm_rows, all_rows),
        out_shape=(
            jax.ShapeDtypeStruct((PG, share, width), F32),
            jax.ShapeDtypeStruct((PG, share), F32),
            jax.ShapeDtypeStruct((2,), F32),
        ),
        in_specs=[vmem] * 3,
        out_specs=(vmem, vmem, pl.BlockSpec(memory_space=pltpu.SMEM)),
    )(*[pltpu.with_memory_space_constraint(a, pltpu.VMEM) for a in sums])


def slot_terms(basis, residual, sigma, counts, pulsar, group_ids, ecorr):
    sig = sigma.astype(jnp.float32)
    res = residual.astype(jnp.float32)
    rowpos = lax.broadcasted_iota(jnp.int32, sig.shape, 2)
    valid = rowpos < counts[..., None]
    inverse = jnp.where(valid, 1.0 / (sig * sig), jnp.float32(0.0))
    weighted = (inverse[..., None] * basis).astype(jnp.bfloat16)
    global_id = group_ids[:, None] * PG + pulsar
    table = jnp.arange(ecorr.shape[0], dtype=jnp.int32)
    chosen = jnp.sum(jnp.where(global_id[..., None] == table, ecorr, jnp.float32(0.0)), axis=-1)
    jitter = chosen * chosen
    total = jnp.sum(inverse, axis=2)
    coef = jitter / (1.0 + jitter * total)
    column = jnp.sum(weighted.astype(jnp.float32), axis=2)
    project = jnp.sum(weighted.astype(jnp.float32) * res[..., None], axis=2)
    wsum = jnp.sum(inverse * res, axis=2)
    chi = jnp.sum(inverse * res * res) - jnp.sum(coef * wsum * wsum)
    logdet = jnp.sum(jnp.where(valid, jnp.log(sig * sig), jnp.float32(0.0))) + jnp.sum(
        jnp.log(1.0 + jitter * total)
    )
    adjusted = project - (coef * wsum)[..., None] * column
    grams = []
    sums = []
    for member in range(PG):
        picked = pulsar == member
        masked = jnp.where(picked[..., None, None], weighted, jnp.zeros((), jnp.bfloat16))
        first = jnp.einsum("gslk,gslm->gkm", basis, masked, preferred_element_type=jnp.float32)
        scale = jnp.where(picked, coef, jnp.float32(0.0))
        minus = jnp.einsum(
            "gs,gsk,gsm->gkm", scale, column, column, precision=lax.Precision.HIGHEST
        )
        grams.append(first - minus)
        sums.append(jnp.sum(jnp.where(picked[..., None], adjusted, jnp.float32(0.0)), axis=1))
    return (jnp.stack(grams, axis=1), jnp.stack(sums, axis=1), logdet, chi)


def on_device(basis, residual, sigma, counts, pulsar, ecorr):
    groups = lax.axis_size("psr")
    ndp = lax.axis_size("dp")
    width = basis.shape[-1]
    rows = basis.shape[-2]
    slots = basis.shape[2]
    share = width // ndp
    group_ids = jnp.arange(groups, dtype=jnp.int32)
    gram, rhs, logdet, chi = slot_terms(
        basis[0], residual[0], sigma[0], counts[0], pulsar[0], group_ids, ecorr
    )
    gram_rows = (
        gram.reshape(groups, PG, ndp, share, width)
        .transpose(2, 0, 1, 3, 4)
        .reshape(ndp * groups * PG * share, width)
    )
    rhs_rows = (
        rhs.reshape(groups, PG, ndp, share).transpose(2, 0, 1, 3).reshape(ndp * groups * PG * share)
    )
    gram_part, rhs_part = (
        lax.psum_scatter(gram_rows, ("dp", "psr"), scatter_dimension=0, tiled=True),
        lax.psum_scatter(rhs_rows, ("dp", "psr"), scatter_dimension=0, tiled=True),
    )
    gram_part = gram_part.reshape(PG, share, width)
    rhs_part = rhs_part.reshape(PG, share)
    summed = lax.psum((logdet, chi), ("dp", "psr"))
    norm_rows = float(ndp * slots * rows)
    all_rows = float(ndp * groups * groups * slots * rows)
    totals = jnp.stack([summed[0], summed[1]]) / all_rows
    return (gram_part / norm_rows, rhs_part / norm_rows, totals)


def solution(mesh):
    def step(basis, *rest):
        groups, _, rows, width = basis.shape[1:]
        ndp = lax.axis_size("dp")
        tiled = ndp % 4 == 0 and width % (16 * ndp) == 0 and width % 256 == 0 and width == 2 * rows
        if groups == lax.axis_size("psr") == 2 * 2 and tiled:
            return fused(basis, *rest)
        return on_device(basis, *rest)

    return jax.shard_map(
        step,
        mesh=mesh,
        in_specs=(
            P(("dp", "psr"), None, None, None, None),
            P(("dp", "psr"), None, None, None),
            P(("dp", "psr"), None, None, None),
            P(("dp", "psr"), None, None),
            P(("dp", "psr"), None, None),
            P(),
        ),
        out_specs=(P("psr", "dp", None), P("psr", "dp"), P()),
        check_vma=False,
    )
```

```python
import functools

import jax
import jax.numpy as jnp
from jax import lax
from jax.experimental import pallas as pl
from jax.experimental.pallas import tpu as pltpu
from jax.sharding import PartitionSpec as P

PG = 4
HOPS = 2
MESH = pl.DeviceIdType.MESH
F32 = jnp.float32
BF16 = jnp.bfloat16


def stack_rows(ref, order):
    return jnp.concatenate([ref[g].astype(F32) for g in order], axis=0)


def columns(ref, order, slots):
    rows = [jnp.broadcast_to(ref[pl.ds(g, 1), :].astype(F32), (slots, slots)) for g in order]
    eye = jnp.concatenate([jnp.where(r == c, F32(1.0), F32(0.0)) for r, c in [triangle(slots)]] * len(order), axis=0)
    return jnp.sum(jnp.concatenate(rows, axis=0) * eye, axis=1, keepdims=True)


def slot_weights(order, res_ref, sig_ref, cnt_ref, pul_ref, ecorr_ref):
    slots, rows = sig_ref.shape[1:]
    n = len(order) * slots
    sig = stack_rows(sig_ref, order)
    res = stack_rows(res_ref, order)
    counts = columns(cnt_ref, order, slots)
    pulsar = columns(pul_ref, order, slots)
    base = jnp.concatenate([jnp.full((slots, 1), (g * PG).astype(F32)) for g in order], axis=0)
    lane = lax.broadcasted_iota(jnp.int32, (n, rows), 1)
    valid = lane.astype(F32) < counts
    var = sig * sig
    inverse = jnp.where(valid, 1.0 / var, F32(0.0))
    total = jnp.sum(inverse, axis=1, keepdims=True)
    n_table = ecorr_ref.shape[1]
    table = lax.broadcasted_iota(jnp.int32, (n, n_table), 1).astype(F32)
    chosen = jnp.sum(
        jnp.where(pulsar + base == table, jnp.broadcast_to(ecorr_ref[...], (n, n_table)), F32(0.0)),
        axis=1,
        keepdims=True,
    )
    jitter = chosen * chosen
    coef = jitter / (1.0 + jitter * total)
    wres = inverse * res
    wsum = jnp.sum(wres, axis=1, keepdims=True)
    first = lane == 0
    chi = wres * res - jnp.where(first, coef * wsum * wsum, F32(0.0))
    logdet = jnp.where(valid, jnp.log(var), F32(0.0)) + jnp.where(
        first, jnp.log(1.0 + jitter * total), F32(0.0)
    )
    tot = jnp.concatenate(
        [jnp.sum(logdet, axis=0, keepdims=True), jnp.sum(chi, axis=0, keepdims=True)], axis=1
    )
    return inverse, wres, coef, coef * wsum, pulsar, tot


def split(value):
    high = value.astype(BF16).astype(F32)
    return high, value - high


def group_left(inverse, wres, pulsar):
    slots, rows = inverse.shape
    slot = lax.broadcasted_iota(jnp.int32, (slots, rows), 0)
    member = lax.broadcasted_iota(jnp.int32, (PG, rows), 0).astype(F32)
    hots = [
        jnp.where(member == jnp.broadcast_to(pulsar[s : s + 1], (PG, rows)), F32(1.0), F32(0.0))
        for s in range(slots)
    ]

    def spread(a):
        return jnp.concatenate([jnp.where(slot == s, a, F32(0.0)) for s in range(slots)], axis=1)

    def hot(a):
        return jnp.concatenate([hots[s] * a[s : s + 1] for s in range(slots)], axis=1)

    left = [spread(a) for a in split(inverse)] + [hot(a) for a in split(wres)]
    return jnp.concatenate(left, axis=0).astype(BF16)


def group_sums(basis, inverse, wres, coef, cw, pulsar, shift_ref):
    slots, rows, width = basis.shape
    left = group_left(inverse, wres, pulsar)
    flat = basis[...].reshape(slots * rows, width)
    half = slots * rows // 2
    sums = jnp.dot(left[:, :half], flat[:half], preferred_element_type=F32) + jnp.dot(
        left[:, half:], flat[half:], preferred_element_type=F32
    )
    column = sums[:slots] + sums[slots : 2 * slots]
    project = sums[2 * slots : 2 * slots + PG] + sums[2 * slots + PG : 2 * slots + 2 * PG]
    minus = jnp.concatenate(
        [
            jnp.sum(jnp.where(pulsar == F32(m), cw, F32(0.0)) * column, axis=0, keepdims=True)
            for m in range(PG)
        ],
        axis=0,
    )
    shift = coef * column
    for s in range(slots):
        shift_ref[s] = jnp.broadcast_to(shift[s : s + 1], shift_ref.shape[1:])
    return project - minus


def slot_order(pulsars):
    rank = [jnp.int32(0)] * len(pulsars)
    for s in range(len(pulsars)):
        for t in range(s):
            before = jnp.where(pulsars[t] <= pulsars[s], 1, 0)
            rank[s] = rank[s] + before
            rank[t] = rank[t] + (1 - before)
    slots = range(len(pulsars))
    perm = [sum(jnp.where(rank[s] == j, s, 0) for s in slots) for j in slots]
    ends = [sum(jnp.where(p <= m, 1, 0) for p in pulsars) for m in range(PG - 1)]
    return perm, [0] + ends + [len(pulsars)]


def running_grams(basis, perm, first, inv_ref, shift_ref, run, run_diag):
    slots, rows, width = basis.shape
    hw = width // 2
    r, c = triangle(hw)
    for j in range(slots):
        s = perm[j]
        block = basis[s]
        centred = (block.astype(F32).reshape(rows // 8, 8, width) - shift_ref[s][None]).reshape(rows, width)
        weighted = (block.T.astype(F32).reshape(width // 8, 8, rows) * inv_ref[first + s][None]).reshape(width, rows)
        full = jnp.dot(weighted.astype(BF16), centred.astype(BF16), preferred_element_type=F32)
        low = full[hw:, hw:]
        cross = full[:hw, hw:]
        both = jnp.where(r <= c, full[:hw, :hw], low)
        diag = jnp.broadcast_to(jnp.sum(jnp.where(r == c, low, F32(0.0)), axis=0, keepdims=True), (8, hw))
        if j:
            cross = cross + run[j, 0]
            both = both + run[j, 1]
            diag = diag + run_diag[j]
        run[j + 1, 0] = cross
        run[j + 1, 1] = both
        run_diag[j + 1] = diag


def triangle(n):
    return lax.broadcasted_iota(jnp.int32, (n, n), 0), lax.broadcasted_iota(jnp.int32, (n, n), 1)


def small_tiles(ref, rhs, diag, tot):
    hw = rhs.shape[1] // 2
    for h in range(2):
        rows = [rhs[:, h * hw : (h + 1) * hw], tot[:, :hw], tot[:, hw:]] + diag[h * PG // 2 : (h + 1) * PG // 2]
        ref[h] = jnp.concatenate(rows, axis=0)


def kernel(
    ndp,
    basis_ref, res_in, sig_in, cnt_in, pul_in, ecorr_in,
    gram_ref, rhs_ref, tot_ref,
    buf0, buf1, buf2, buf3, res_ref, sig_ref, cnt_ref, pul_ref, ecorr_ref, ids_ref,
    run0, run1, run2, run3, diag0, diag1, diag2, diag3, inv_ref, shift0, shift1, shift2, shift3,
    out_c, in_c, out_f, out_n, in_p, out_d, in_d, acc, out_h, in_h,
    s_core, r_core, s_near, s_far, r_p, s_z, r_z,
    load_sem, send_sem, recv_sem,
):
    nz = ndp // 2
    dp = lax.axis_index("dp")
    psr = lax.axis_index("psr")
    c, y = psr % 2, psr // 2
    x, z = dp % 2, dp // 2
    c2, y2, x2 = 1 - c, 1 - y, 1 - x
    core_peer = (dp, y * 2 + c2)
    y_peer = (dp, y2 * 2 + c)
    x_peer = (z * 2 + x2, psr)
    xy_peer = (z * 2 + x2, y2 * 2 + c)
    steps = [(k, j) for k in range(1, nz) for j in range(2)] + [(0, 1)]
    dp_peers = {(k, j): (((z + k) % nz) * 2 + (x + j) % 2, psr) for k, j in steps}
    order = (y2 * 2 + c2, y2 * 2 + c, y * 2 + c2, psr)
    bufs = (buf0, buf1, buf2, buf3)
    runs = (run0, run1, run2, run3)
    diags = (diag0, diag1, diag2, diag3)
    shifts = (shift0, shift1, shift2, shift3)

    barrier = pltpu.get_barrier_semaphore()
    greeted = [core_peer, y_peer, xy_peer] + list(dp_peers.values())
    for peer in greeted:
        pl.semaphore_signal(barrier, inc=1, device_id=peer, device_id_type=MESH)
    small_loads = []
    pairs = ((sig_in, sig_ref), (cnt_in, cnt_ref), (pul_in, ids_ref), (res_in, res_ref), (pul_in, pul_ref))
    for i, (src, dst) in enumerate(pairs + ((ecorr_in, ecorr_ref),)):
        load = pltpu.make_async_copy(src, dst, load_sem.at[len(order) + i])
        load.start()
        small_loads.append(load)
    loads = []
    for i, g in enumerate(order):
        load = pltpu.make_async_copy(basis_ref.at[g], bufs[i], load_sem.at[i])
        load.start()
        loads.append(load)

    arrivals, departures = {}, {}

    def send(src, dst, peer, arrival, departure):
        copy = pltpu.make_async_remote_copy(
            src_ref=src, dst_ref=dst,
            send_sem=send_sem.at[departures.setdefault(departure, len(departures))],
            recv_sem=recv_sem.at[arrivals.setdefault(arrival, len(arrivals))],
            device_id=peer, device_id_type=MESH,
        )
        copy.start()

    def arrived(arrival, whole):
        pltpu.make_async_remote_copy(
            src_ref=whole, dst_ref=whole, send_sem=send_sem.at[0], recv_sem=recv_sem.at[arrivals[arrival]],
            device_id=core_peer, device_id_type=MESH,
        ).wait_recv()

    def departed(departure, whole):
        pltpu.make_async_remote_copy(
            src_ref=whole, dst_ref=whole, send_sem=send_sem.at[departures[departure]], recv_sem=recv_sem.at[0],
            device_id=core_peer, device_id_type=MESH,
        ).wait_send()

    for load in small_loads:
        load.wait()
    slots = sig_ref.shape[1]
    inverse, wres, coef, cw, pulsar, tot = slot_weights(order, res_ref, sig_ref, cnt_ref, pul_ref, ecorr_ref)

    for i in range(len(order) * slots):
        inv_ref[i] = jnp.broadcast_to(inverse[i : i + 1], inv_ref.shape[1:])
    for i in range(len(order)):
        runs[i][0] = jnp.zeros(runs[i].shape[1:], F32)
        diags[i][0] = jnp.zeros(diags[i].shape[1:], F32)
    rhs, ends = {}, {}

    def head(i):
        mine = slice(i * slots, (i + 1) * slots)
        rhs[i] = group_sums(
            bufs[i], inverse[mine], wres[mine], coef[mine], cw[mine], pulsar[mine], shifts[i]
        )

    def grams(i):
        perm, ends[i] = slot_order([ids_ref[order[i], s] for s in range(slots)])
        running_grams(bufs[i], perm, i * slots, inv_ref, shifts[i], runs[i], diags[i])

    def member(i, m, h):
        value = runs[i][ends[i][m + 1], h]
        return value - runs[i][ends[i][m], h] if m else value

    def small(ref, i):
        rows = [diags[i][e][:1] for e in ends[i]]
        small_tiles(ref, rhs[i], [rows[m + 1] - rows[m] for m in range(PG)], tot)

    def to_core(n, i):
        small(s_core.at[n], i)
        for m in range(PG):
            for h in range(2):
                out_c[n * PG + m, h] = member(i, m, h).astype(BF16)

    def core_sends(n):
        send(s_core.at[n], r_core.at[n], core_peer, ("core small", n), "core small")
        for m in range(PG):
            key = "near" if n else ("far", min(m, 1))
            send(out_c.at[n * PG + m], in_c.at[n * PG + m], core_peer, key, "core")

    loads[0].wait()
    head(0)
    grams(0)
    to_core(0, 0)
    pl.semaphore_wait(barrier, len(greeted))
    core_sends(0)
    for load in loads[1:]:
        load.wait()
    head(1)
    head(2)
    head(3)
    grams(1)
    grams(2)
    to_core(1, 2)
    core_sends(1)
    small(s_far, 1)
    arrived(("core small", 0), r_core.at[0])
    s_far[...] = s_far[...] + r_core[0]
    send(s_far, r_p.at[0], y_peer, "small", "small")
    send(s_far, r_p.at[1], xy_peer, "small", "small")
    def far_sum(m):
        if m == 0:
            arrived(("far", 0), in_c.at[0])
        if m == 1:
            arrived(("far", 1), in_c.at[pl.ds(1, PG - 1)])
        for h in range(2):
            out_f[m, h] = (member(1, m, h) + in_c[m, h].astype(F32)).astype(BF16)

    def to_y(m):
        send(out_f.at[m, x], in_p.at[m, 0], y_peer, ("plane", m), "far")

    def to_xy(m):
        send(out_f.at[m, x2], in_p.at[m, 1], xy_peer, ("plane", m), "far")

    def to_x(m):
        out_n[m] = (member(3, m, x2) + in_c[PG + m, x2].astype(F32)).astype(BF16)
        send(out_n.at[m], in_p.at[m, 2], x_peer, ("plane", m), "near")

    far_sum(0)
    to_y(0)
    far_sum(1)
    to_y(1)
    to_xy(0)
    far_sum(2)
    to_y(2)
    far_sum(3)
    to_y(3)
    grams(3)
    small(s_near, 3)
    arrived(("core small", 1), r_core.at[1])
    arrived("near", in_c.at[pl.ds(PG, PG)])
    s_near[...] = s_near[...] + r_core[1]
    send(s_near, r_p.at[2], x_peer, "small", "small")
    to_x(0)
    to_xy(1)
    to_x(1)
    to_xy(2)
    to_x(2)
    to_xy(3)
    to_x(3)

    total = s_near[...]
    arrived("small", r_p)
    for i in range(3):
        total = total + r_p[i]
    s_z[...] = total
    hz = nz // 2
    for k in range(1, nz):
        send(s_z.at[((z + k) % nz) // hz], r_z.at[k - 1], dp_peers[k, 0], "small z", "small z")

    hw = out_n.shape[1]
    row, col = triangle(hw)
    crossed = x == 0
    upper = jnp.logical_or(row <= col, crossed)
    lower = jnp.logical_and(row > col, jnp.logical_not(crossed))
    middle = jnp.logical_and(row == col, jnp.logical_not(crossed))

    def to_all(m):
        value = member(3, m, x) + in_c[PG + m, x].astype(F32)
        arrived(("plane", m), in_p.at[m])
        for i in range(3):
            value = value + in_p[m, i].astype(F32)
        value = value.astype(BF16)
        turned = value.T.astype(F32)
        value = value.astype(F32)
        at = PG + 2 + m % (PG // 2)
        diag = jnp.broadcast_to(total[m // (PG // 2), at : at + 1], (hw, hw))
        top = jnp.where(upper, value, turned)
        low = jnp.where(lower, value, jnp.where(middle, diag, turned))
        out_d[m] = jnp.concatenate([top, low], axis=0).astype(BF16).reshape(out_d.shape[1:])
        for k in range(1, nz):
            if m < HOPS:
                send(out_d.at[m, (z + k) % nz], in_d.at[m, k], dp_peers[k, 0], ("z", m), "z")
        if m >= HOPS:
            for k, j in steps:
                keys = (("z", m), "z") if k else (("x", m), "x")
                send(out_d.at[m, (z + k) % nz, (x + j) % 2], in_d.at[m, k, j], dp_peers[k, j], *keys)

    def hop(m):
        both = out_d[m, z].astype(F32)
        arrived(("z", m), in_d.at[m, pl.ds(1, nz - 1)])
        for k in range(1, nz):
            both = both + in_d[m, k].astype(F32)
        acc[m] = both
        out_h[m] = acc[m, x2].astype(BF16)
        send(out_h.at[m], in_h.at[m], x_peer, "hop", "hop")

    def finish(m):
        if m < HOPS:
            if m == 0:
                arrived("hop", in_h)
            own = acc[m, x]
            other = in_h[m].astype(F32)
        else:
            own = out_d[m, z, x].astype(F32)
            arrived(("x", m), in_d.at[m, 0, 1])
            arrived(("z", m), in_d.at[m, pl.ds(1, nz - 1)])
            for k in range(1, nz):
                own = own + in_d[m, k, 0].astype(F32)
            other = in_d[m, 0, 1].astype(F32)
            for k in range(1, nz):
                other = other + in_d[m, k, 1].astype(F32)
        swap = (x + z // hz) % 2 == 0
        left = jnp.where(swap, other, own)
        gram_ref[m] = jnp.concatenate([left, jnp.where(swap, own, other)], axis=1)

    for m in range(PG):
        to_all(m)
    for m in range(HOPS):
        hop(m)
    for m in range(PG - 1):
        finish(m)
    final = s_z[z // hz]
    arrived("small z", r_z)
    for k in range(1, nz):
        final = final + r_z[k - 1]
    share = rhs_ref.shape[1]
    mine = jnp.zeros((PG, share), F32)
    for e in range(hw // share):
        mine = mine + jnp.where(dp % (hw // share) == e, final[:PG, e * share : (e + 1) * share], F32(0.0))
    rhs_ref[...] = mine
    tot_ref[...] = jnp.concatenate([final[PG : PG + 1], final[PG + 1 : PG + 2]], axis=1)
    finish(PG - 1)
    wholes = {
        "core small": s_core, "core": out_c, "far": out_f, "near": out_n, "small": r_p, "small z": r_z,
        "z": out_d.at[:, pl.ds(1, nz - 1)], "x": out_d.at[pl.ds(HOPS, PG - HOPS), 0, 0], "hop": out_h,
    }
    for departure in departures:
        departed(departure, wholes[departure])


def scale_kernel(norm_rows, all_rows, gram_in, rhs_in, tot_in, gram_ref, rhs_ref, tot_ref):
    gram_ref[...] = gram_in[...] / norm_rows
    rhs_ref[...] = rhs_in[...] / norm_rows
    rows = tot_in.shape[1] // 2
    tot_ref[0] = jnp.sum(tot_in[:, :rows]) / all_rows
    tot_ref[1] = jnp.sum(tot_in[:, rows:]) / all_rows


def fused(basis, residual, sigma, counts, pulsar, ecorr):
    ndp = lax.axis_size("dp")
    groups, slots, rows, width = basis.shape[1:]
    share = width // ndp
    nz = ndp // 2
    norm_rows = float(ndp * slots * rows)
    all_rows = float(ndp * groups * groups * slots * rows)
    vmem = pl.BlockSpec(memory_space=pltpu.VMEM)
    hw = width // 2
    tile = (2, 2 * PG, hw)
    n_arrivals = 2 + 3 + PG + 1 + 1 + PG + (PG - HOPS) + 1
    sums = pl.pallas_call(
        functools.partial(kernel, ndp),
        out_shape=(
            pltpu.VMEM((PG, share, width), F32),
            pltpu.VMEM((PG, share), F32),
            pltpu.VMEM((1, 2 * rows), F32),
        ),
        in_specs=[pl.BlockSpec(memory_space=pltpu.HBM)] * 6,
        out_specs=(vmem, vmem, vmem),
        scratch_shapes=[
            pltpu.VMEM((slots, rows, width), BF16),
            pltpu.VMEM((slots, rows, width), BF16),
            pltpu.VMEM((slots, rows, width), BF16),
            pltpu.VMEM((slots, rows, width), BF16),
            pltpu.VMEM((groups, slots, rows), BF16),
            pltpu.VMEM((groups, slots, rows), BF16),
            pltpu.VMEM((groups, slots), jnp.int32),
            pltpu.VMEM((groups, slots), jnp.int32),
            pltpu.VMEM((1, ecorr.shape[0]), F32),
            pltpu.SMEM((groups, slots), jnp.int32),
            *[pltpu.VMEM((slots + 1, 2, hw, hw), F32)] * groups,
            *[pltpu.VMEM((slots + 1, 8, hw), F32)] * groups,
            pltpu.VMEM((groups * slots, 8, rows), F32),
            *[pltpu.VMEM((slots, 8, width), F32)] * groups,
            pltpu.VMEM((2 * PG, 2, hw, hw), BF16),
            pltpu.VMEM((2 * PG, 2, hw, hw), BF16),
            pltpu.VMEM((PG, 2, hw, hw), BF16),
            pltpu.VMEM((PG, hw, hw), BF16),
            pltpu.VMEM((PG, 3, hw, hw), BF16),
            pltpu.VMEM((PG, nz, 2, share, hw), BF16),
            pltpu.VMEM((PG, nz, 2, share, hw), BF16),
            pltpu.VMEM((HOPS, 2, share, hw), F32),
            pltpu.VMEM((HOPS, share, hw), BF16),
            pltpu.VMEM((HOPS, share, hw), BF16),
            pltpu.VMEM((2,) + tile, F32),
            pltpu.VMEM((2,) + tile, F32),
            pltpu.VMEM(tile, F32),
            pltpu.VMEM(tile, F32),
            pltpu.VMEM((3,) + tile, F32),
            pltpu.VMEM(tile, F32),
            pltpu.VMEM((nz - 1,) + tile[1:], F32),
            pltpu.SemaphoreType.DMA((groups + 6,)),
            pltpu.SemaphoreType.DMA((9,)),
            pltpu.SemaphoreType.DMA((n_arrivals,)),
        ],
        compiler_params=pltpu.CompilerParams(
            collective_id=0, has_side_effects=True
        ),
    )(basis[0], residual[0], sigma[0], counts[0], pulsar[0], ecorr.reshape(1, -1))
    return pl.pallas_call(
        functools.partial(scale_kernel, norm_rows, all_rows),
        out_shape=(
            jax.ShapeDtypeStruct((PG, share, width), F32),
            jax.ShapeDtypeStruct((PG, share), F32),
            jax.ShapeDtypeStruct((2,), F32),
        ),
        in_specs=[vmem] * 3,
        out_specs=(vmem, vmem, pl.BlockSpec(memory_space=pltpu.SMEM)),
    )(*[pltpu.with_memory_space_constraint(a, pltpu.VMEM) for a in sums])


def slot_terms(basis, residual, sigma, counts, pulsar, group_ids, ecorr):
    sig = sigma.astype(jnp.float32)
    res = residual.astype(jnp.float32)
    rowpos = lax.broadcasted_iota(jnp.int32, sig.shape, 2)
    valid = rowpos < counts[..., None]
    inverse = jnp.where(valid, 1.0 / (sig * sig), jnp.float32(0.0))
    weighted = (inverse[..., None] * basis).astype(jnp.bfloat16)
    global_id = group_ids[:, None] * PG + pulsar
    table = jnp.arange(ecorr.shape[0], dtype=jnp.int32)
    chosen = jnp.sum(jnp.where(global_id[..., None] == table, ecorr, jnp.float32(0.0)), axis=-1)
    jitter = chosen * chosen
    total = jnp.sum(inverse, axis=2)
    coef = jitter / (1.0 + jitter * total)
    column = jnp.sum(weighted.astype(jnp.float32), axis=2)
    project = jnp.sum(weighted.astype(jnp.float32) * res[..., None], axis=2)
    wsum = jnp.sum(inverse * res, axis=2)
    chi = jnp.sum(inverse * res * res) - jnp.sum(coef * wsum * wsum)
    logdet = jnp.sum(jnp.where(valid, jnp.log(sig * sig), jnp.float32(0.0))) + jnp.sum(
        jnp.log(1.0 + jitter * total)
    )
    adjusted = project - (coef * wsum)[..., None] * column
    grams = []
    sums = []
    for member in range(PG):
        picked = pulsar == member
        masked = jnp.where(picked[..., None, None], weighted, jnp.zeros((), jnp.bfloat16))
        first = jnp.einsum("gslk,gslm->gkm", basis, masked, preferred_element_type=jnp.float32)
        scale = jnp.where(picked, coef, jnp.float32(0.0))
        minus = jnp.einsum(
            "gs,gsk,gsm->gkm", scale, column, column, precision=lax.Precision.HIGHEST
        )
        grams.append(first - minus)
        sums.append(jnp.sum(jnp.where(picked[..., None], adjusted, jnp.float32(0.0)), axis=1))
    return (jnp.stack(grams, axis=1), jnp.stack(sums, axis=1), logdet, chi)


def on_device(basis, residual, sigma, counts, pulsar, ecorr):
    groups = lax.axis_size("psr")
    ndp = lax.axis_size("dp")
    width = basis.shape[-1]
    rows = basis.shape[-2]
    slots = basis.shape[2]
    share = width // ndp
    group_ids = jnp.arange(groups, dtype=jnp.int32)
    gram, rhs, logdet, chi = slot_terms(
        basis[0], residual[0], sigma[0], counts[0], pulsar[0], group_ids, ecorr
    )
    gram_rows = (
        gram.reshape(groups, PG, ndp, share, width)
        .transpose(2, 0, 1, 3, 4)
        .reshape(ndp * groups * PG * share, width)
    )
    rhs_rows = (
        rhs.reshape(groups, PG, ndp, share).transpose(2, 0, 1, 3).reshape(ndp * groups * PG * share)
    )
    gram_part, rhs_part = (
        lax.psum_scatter(gram_rows, ("dp", "psr"), scatter_dimension=0, tiled=True),
        lax.psum_scatter(rhs_rows, ("dp", "psr"), scatter_dimension=0, tiled=True),
    )
    gram_part = gram_part.reshape(PG, share, width)
    rhs_part = rhs_part.reshape(PG, share)
    summed = lax.psum((logdet, chi), ("dp", "psr"))
    norm_rows = float(ndp * slots * rows)
    all_rows = float(ndp * groups * groups * slots * rows)
    totals = jnp.stack([summed[0], summed[1]]) / all_rows
    return (gram_part / norm_rows, rhs_part / norm_rows, totals)


def solution(mesh):
    def step(basis, *rest):
        groups, _, rows, width = basis.shape[1:]
        ndp = lax.axis_size("dp")
        tiled = ndp % 4 == 0 and width % (16 * ndp) == 0 and width % 256 == 0 and width == 2 * rows
        if groups == lax.axis_size("psr") == 2 * 2 and tiled:
            return fused(basis, *rest)
        return on_device(basis, *rest)

    return jax.shard_map(
        step,
        mesh=mesh,
        in_specs=(
            P(("dp", "psr"), None, None, None, None),
            P(("dp", "psr"), None, None, None),
            P(("dp", "psr"), None, None, None),
            P(("dp", "psr"), None, None),
            P(("dp", "psr"), None, None),
            P(),
        ),
        out_specs=(P("psr", "dp", None), P("psr", "dp"), P()),
        check_vma=False,
    )
```

```python
import functools

import jax
import jax.numpy as jnp
from jax import lax
from jax.experimental import pallas as pl
from jax.experimental.pallas import tpu as pltpu
from jax.sharding import PartitionSpec as P

PG = 4
HOPS = 2
MESH = pl.DeviceIdType.MESH
F32 = jnp.float32
BF16 = jnp.bfloat16


def stack_rows(ref, order):
    return jnp.concatenate([ref[g].astype(F32) for g in order], axis=0)


def columns(ref, order, slots):
    rows = [jnp.broadcast_to(ref[pl.ds(g, 1), :].astype(F32), (slots, slots)) for g in order]
    eye = jnp.concatenate([jnp.where(r == c, F32(1.0), F32(0.0)) for r, c in [triangle(slots)]] * len(order), axis=0)
    return jnp.sum(jnp.concatenate(rows, axis=0) * eye, axis=1, keepdims=True)


def slot_weights(order, res_ref, sig_ref, cnt_ref, pul_ref, ecorr_ref):
    slots, rows = sig_ref.shape[1:]
    n = len(order) * slots
    sig = stack_rows(sig_ref, order)
    res = stack_rows(res_ref, order)
    counts = columns(cnt_ref, order, slots)
    pulsar = columns(pul_ref, order, slots)
    base = jnp.concatenate([jnp.full((slots, 1), (g * PG).astype(F32)) for g in order], axis=0)
    lane = lax.broadcasted_iota(jnp.int32, (n, rows), 1)
    valid = lane.astype(F32) < counts
    var = sig * sig
    inverse = jnp.where(valid, 1.0 / var, F32(0.0))
    total = jnp.sum(inverse, axis=1, keepdims=True)
    n_table = ecorr_ref.shape[1]
    table = lax.broadcasted_iota(jnp.int32, (n, n_table), 1).astype(F32)
    chosen = jnp.sum(
        jnp.where(pulsar + base == table, jnp.broadcast_to(ecorr_ref[...], (n, n_table)), F32(0.0)),
        axis=1,
        keepdims=True,
    )
    jitter = chosen * chosen
    coef = jitter / (1.0 + jitter * total)
    wres = inverse * res
    wsum = jnp.sum(wres, axis=1, keepdims=True)
    first = lane == 0
    chi = wres * res - jnp.where(first, coef * wsum * wsum, F32(0.0))
    logdet = jnp.where(valid, jnp.log(var), F32(0.0)) + jnp.where(
        first, jnp.log(1.0 + jitter * total), F32(0.0)
    )
    tot = jnp.concatenate(
        [jnp.sum(logdet, axis=0, keepdims=True), jnp.sum(chi, axis=0, keepdims=True)], axis=1
    )
    return inverse, wres, coef, coef * wsum, pulsar, tot


def split(value):
    high = value.astype(BF16).astype(F32)
    return high, value - high


def group_left(inverse, wres, pulsar):
    slots, rows = inverse.shape
    slot = lax.broadcasted_iota(jnp.int32, (slots, rows), 0)
    member = lax.broadcasted_iota(jnp.int32, (PG, rows), 0).astype(F32)
    hots = [
        jnp.where(member == jnp.broadcast_to(pulsar[s : s + 1], (PG, rows)), F32(1.0), F32(0.0))
        for s in range(slots)
    ]

    def spread(a):
        return jnp.concatenate([jnp.where(slot == s, a, F32(0.0)) for s in range(slots)], axis=1)

    def hot(a):
        return jnp.concatenate([hots[s] * a[s : s + 1] for s in range(slots)], axis=1)

    left = [spread(a) for a in split(inverse)] + [hot(a) for a in split(wres)]
    return jnp.concatenate(left, axis=0).astype(BF16)


def group_sums(basis, inverse, wres, coef, cw, pulsar, shift_ref):
    slots, rows, width = basis.shape
    left = group_left(inverse, wres, pulsar)
    flat = basis[...].reshape(slots * rows, width)
    half = slots * rows // 2
    sums = jnp.dot(left[:, :half], flat[:half], preferred_element_type=F32) + jnp.dot(
        left[:, half:], flat[half:], preferred_element_type=F32
    )
    column = sums[:slots] + sums[slots : 2 * slots]
    project = sums[2 * slots : 2 * slots + PG] + sums[2 * slots + PG : 2 * slots + 2 * PG]
    minus = jnp.concatenate(
        [
            jnp.sum(jnp.where(pulsar == F32(m), cw, F32(0.0)) * column, axis=0, keepdims=True)
            for m in range(PG)
        ],
        axis=0,
    )
    shift = coef * column
    for s in range(slots):
        shift_ref[s] = jnp.broadcast_to(shift[s : s + 1], shift_ref.shape[1:])
    return project - minus


def slot_order(pulsars):
    rank = [jnp.int32(0)] * len(pulsars)
    for s in range(len(pulsars)):
        for t in range(s):
            before = jnp.where(pulsars[t] <= pulsars[s], 1, 0)
            rank[s] = rank[s] + before
            rank[t] = rank[t] + (1 - before)
    slots = range(len(pulsars))
    perm = [sum(jnp.where(rank[s] == j, s, 0) for s in slots) for j in slots]
    ends = [sum(jnp.where(p <= m, 1, 0) for p in pulsars) for m in range(PG - 1)]
    return perm, [0] + ends + [len(pulsars)]


def running_grams(basis, perm, first, inv_ref, shift_ref, run, run_diag):
    slots, rows, width = basis.shape
    hw = width // 2
    r, c = triangle(hw)
    for j in range(slots):
        s = perm[j]
        block = basis[s]
        centred = (block.astype(F32).reshape(rows // 8, 8, width) - shift_ref[s][None]).reshape(rows, width)
        weighted = (block.T.astype(F32).reshape(width // 8, 8, rows) * inv_ref[first + s][None]).reshape(width, rows)
        weighted, centred = weighted.astype(BF16), centred.astype(BF16)
        top = jnp.dot(weighted[:hw], centred, preferred_element_type=F32)
        low = jnp.dot(weighted[hw:], centred[:, hw:], preferred_element_type=F32)
        cross = top[:, hw:]
        both = jnp.where(r <= c, top[:, :hw], low)
        diag = jnp.broadcast_to(jnp.sum(jnp.where(r == c, low, F32(0.0)), axis=0, keepdims=True), (8, hw))
        if j:
            cross = cross + run[j, 0]
            both = both + run[j, 1]
            diag = diag + run_diag[j]
        run[j + 1, 0] = cross
        run[j + 1, 1] = both
        run_diag[j + 1] = diag


def triangle(n):
    return lax.broadcasted_iota(jnp.int32, (n, n), 0), lax.broadcasted_iota(jnp.int32, (n, n), 1)


def small_tiles(ref, rhs, diag, tot):
    hw = rhs.shape[1] // 2
    for h in range(2):
        rows = [rhs[:, h * hw : (h + 1) * hw], tot[:, :hw], tot[:, hw:]] + diag[h * PG // 2 : (h + 1) * PG // 2]
        ref[h] = jnp.concatenate(rows, axis=0)


def kernel(
    ndp,
    basis_ref, res_in, sig_in, cnt_in, pul_in, ecorr_in,
    gram_ref, rhs_ref, tot_ref,
    buf0, buf1, buf2, buf3, res_ref, sig_ref, cnt_ref, pul_ref, ecorr_ref, ids_ref,
    run0, run1, run2, run3, diag0, diag1, diag2, diag3, inv_ref, shift0, shift1, shift2, shift3,
    out_c, in_c, out_f, out_n, in_p, out_d, in_d, acc, out_h, in_h,
    s_core, r_core, s_near, s_far, r_p, s_z, r_z,
    load_sem, send_sem, recv_sem,
):
    nz = ndp // 2
    dp = lax.axis_index("dp")
    psr = lax.axis_index("psr")
    c, y = psr % 2, psr // 2
    x, z = dp % 2, dp // 2
    c2, y2, x2 = 1 - c, 1 - y, 1 - x
    core_peer = (dp, y * 2 + c2)
    y_peer = (dp, y2 * 2 + c)
    x_peer = (z * 2 + x2, psr)
    xy_peer = (z * 2 + x2, y2 * 2 + c)
    steps = [(k, j) for k in range(1, nz) for j in range(2)] + [(0, 1)]
    dp_peers = {(k, j): (((z + k) % nz) * 2 + (x + j) % 2, psr) for k, j in steps}
    order = (y2 * 2 + c2, y2 * 2 + c, y * 2 + c2, psr)
    bufs = (buf0, buf1, buf2, buf3)
    runs = (run0, run1, run2, run3)
    diags = (diag0, diag1, diag2, diag3)
    shifts = (shift0, shift1, shift2, shift3)

    barrier = pltpu.get_barrier_semaphore()
    greeted = [core_peer, y_peer, xy_peer] + list(dp_peers.values())
    small_loads = []
    pairs = ((sig_in, sig_ref), (cnt_in, cnt_ref), (pul_in, ids_ref), (res_in, res_ref), (pul_in, pul_ref))
    for i, (src, dst) in enumerate(pairs + ((ecorr_in, ecorr_ref),)):
        load = pltpu.make_async_copy(src, dst, load_sem.at[2 + i])
        load.start()
        small_loads.append(load)
    loads = []
    for i, g in enumerate(order):
        load = pltpu.make_async_copy(basis_ref.at[g], bufs[i], load_sem.at[min(i, 1)])
        load.start()
        loads.append(load)

    for peer in greeted:
        pl.semaphore_signal(barrier, inc=1, device_id=peer, device_id_type=MESH)
    arrivals, departures = {}, {}

    def send(src, dst, peer, arrival, departure):
        copy = pltpu.make_async_remote_copy(
            src_ref=src, dst_ref=dst,
            send_sem=send_sem.at[departures.setdefault(departure, len(departures))],
            recv_sem=recv_sem.at[arrivals.setdefault(arrival, len(arrivals))],
            device_id=peer, device_id_type=MESH,
        )
        copy.start()

    def arrived(arrival, whole):
        pltpu.make_async_remote_copy(
            src_ref=whole, dst_ref=whole, send_sem=send_sem.at[0], recv_sem=recv_sem.at[arrivals[arrival]],
            device_id=core_peer, device_id_type=MESH,
        ).wait_recv()

    def departed(departure, whole):
        pltpu.make_async_remote_copy(
            src_ref=whole, dst_ref=whole, send_sem=send_sem.at[departures[departure]], recv_sem=recv_sem.at[0],
            device_id=core_peer, device_id_type=MESH,
        ).wait_send()

    for load in small_loads:
        load.wait()
    loads[0].wait()
    slots = sig_ref.shape[1]
    inverse, wres, coef, cw, pulsar, tot = slot_weights(order, res_ref, sig_ref, cnt_ref, pul_ref, ecorr_ref)

    for i in range(len(order) * slots):
        inv_ref[i] = jnp.broadcast_to(inverse[i : i + 1], inv_ref.shape[1:])
    for i in range(len(order)):
        runs[i][0] = jnp.zeros(runs[i].shape[1:], F32)
        diags[i][0] = jnp.zeros(diags[i].shape[1:], F32)
    rhs, ends = {}, {}

    def head(i):
        mine = slice(i * slots, (i + 1) * slots)
        rhs[i] = group_sums(
            bufs[i], inverse[mine], wres[mine], coef[mine], cw[mine], pulsar[mine], shifts[i]
        )

    def grams(i):
        perm, ends[i] = slot_order([ids_ref[order[i], s] for s in range(slots)])
        running_grams(bufs[i], perm, i * slots, inv_ref, shifts[i], runs[i], diags[i])

    def member(i, m, h):
        value = runs[i][ends[i][m + 1], h]
        return value - runs[i][ends[i][m], h] if m else value

    def small(ref, i):
        rows = [diags[i][e][:1] for e in ends[i]]
        small_tiles(ref, rhs[i], [rows[m + 1] - rows[m] for m in range(PG)], tot)

    def to_core(n, i):
        small(s_core.at[n], i)
        for m in range(PG):
            for h in range(2):
                out_c[n * PG + m, h] = member(i, m, h).astype(BF16)

    def core_sends(n):
        send(s_core.at[n], r_core.at[n], core_peer, ("core small", n), "core small")
        for m in range(PG):
            key = "near" if n else ("far", min(m, 1))
            send(out_c.at[n * PG + m], in_c.at[n * PG + m], core_peer, key, "core")

    head(0)
    grams(0)
    to_core(0, 0)
    pl.semaphore_wait(barrier, len(greeted))
    core_sends(0)
    rest = basis_ref.at[pl.ds(1, len(loads) - 1)]
    pltpu.make_async_copy(rest, rest, load_sem.at[1]).wait()
    head(1)
    head(2)
    head(3)
    grams(1)
    grams(2)
    to_core(1, 2)
    core_sends(1)
    small(s_far, 1)
    arrived(("core small", 0), r_core.at[0])
    s_far[...] = s_far[...] + r_core[0]
    send(s_far, r_p.at[0], y_peer, "small", "small")
    send(s_far, r_p.at[1], xy_peer, "small", "small")
    def far_sum(m):
        if m == 0:
            arrived(("far", 0), in_c.at[0])
        if m == 1:
            arrived(("far", 1), in_c.at[pl.ds(1, PG - 1)])
        for h in range(2):
            out_f[m, h] = (member(1, m, h) + in_c[m, h].astype(F32)).astype(BF16)

    def to_y(m):
        send(out_f.at[m, x], in_p.at[m, 0], y_peer, ("plane", m), "far")

    def to_xy(m):
        send(out_f.at[m, x2], in_p.at[m, 1], xy_peer, ("plane", m), "far")

    def to_x(m):
        out_n[m] = (member(3, m, x2) + in_c[PG + m, x2].astype(F32)).astype(BF16)
        send(out_n.at[m], in_p.at[m, 2], x_peer, ("plane", m), "near")

    far_sum(0)
    to_y(0)
    far_sum(1)
    to_y(1)
    to_xy(0)
    far_sum(2)
    to_y(2)
    far_sum(3)
    to_y(3)
    grams(3)
    small(s_near, 3)
    arrived(("core small", 1), r_core.at[1])
    arrived("near", in_c.at[pl.ds(PG, PG)])
    s_near[...] = s_near[...] + r_core[1]
    send(s_near, r_p.at[2], x_peer, "small", "small")
    to_x(0)
    to_xy(1)
    to_x(1)
    to_xy(2)
    to_x(2)
    to_xy(3)
    to_x(3)

    total = s_near[...]
    arrived("small", r_p)
    for i in range(3):
        total = total + r_p[i]
    s_z[...] = total
    hz = nz // 2
    for k in range(1, nz):
        send(s_z.at[((z + k) % nz) // hz], r_z.at[k - 1], dp_peers[k, 0], "small z", "small z")

    hw = out_n.shape[1]
    row, col = triangle(hw)
    crossed = x == 0
    upper = jnp.logical_or(row <= col, crossed)
    lower = jnp.logical_and(row > col, jnp.logical_not(crossed))
    middle = jnp.logical_and(row == col, jnp.logical_not(crossed))

    def to_all(m):
        value = member(3, m, x) + in_c[PG + m, x].astype(F32)
        arrived(("plane", m), in_p.at[m])
        for i in range(3):
            value = value + in_p[m, i].astype(F32)
        value = value.astype(BF16)
        turned = value.T.astype(F32)
        value = value.astype(F32)
        at = PG + 2 + m % (PG // 2)
        diag = jnp.broadcast_to(total[m // (PG // 2), at : at + 1], (hw, hw))
        top = jnp.where(upper, value, turned)
        low = jnp.where(lower, value, jnp.where(middle, diag, turned))
        out_d[m] = jnp.concatenate([top, low], axis=0).astype(BF16).reshape(out_d.shape[1:])
        for k in range(1, nz):
            if m < HOPS:
                send(out_d.at[m, (z + k) % nz], in_d.at[m, k], dp_peers[k, 0], ("z", m), "z")
        if m >= HOPS:
            for k, j in steps:
                keys = (("z", m), "z") if k else (("x", m), "x")
                send(out_d.at[m, (z + k) % nz, (x + j) % 2], in_d.at[m, k, j], dp_peers[k, j], *keys)

    def hop(m):
        both = out_d[m, z].astype(F32)
        arrived(("z", m), in_d.at[m, pl.ds(1, nz - 1)])
        for k in range(1, nz):
            both = both + in_d[m, k].astype(F32)
        acc[m] = both
        out_h[m] = acc[m, x2].astype(BF16)
        send(out_h.at[m], in_h.at[m], x_peer, "hop", "hop")

    def finish(m):
        if m < HOPS:
            if m == 0:
                arrived("hop", in_h)
            own = acc[m, x]
            other = in_h[m].astype(F32)
        else:
            own = out_d[m, z, x].astype(F32)
            arrived(("x", m), in_d.at[m, 0, 1])
            arrived(("z", m), in_d.at[m, pl.ds(1, nz - 1)])
            for k in range(1, nz):
                own = own + in_d[m, k, 0].astype(F32)
            other = in_d[m, 0, 1].astype(F32)
            for k in range(1, nz):
                other = other + in_d[m, k, 1].astype(F32)
        swap = (x + z // hz) % 2 == 0
        left = jnp.where(swap, other, own)
        gram_ref[m] = jnp.concatenate([left, jnp.where(swap, own, other)], axis=1)

    for m in range(PG):
        to_all(m)
    for m in range(HOPS):
        hop(m)
    for m in range(PG - 1):
        finish(m)
    final = s_z[z // hz]
    arrived("small z", r_z)
    for k in range(1, nz):
        final = final + r_z[k - 1]
    share = rhs_ref.shape[1]
    mine = jnp.zeros((PG, share), F32)
    for e in range(hw // share):
        mine = mine + jnp.where(dp % (hw // share) == e, final[:PG, e * share : (e + 1) * share], F32(0.0))
    rhs_ref[...] = mine
    tot_ref[...] = jnp.concatenate([final[PG : PG + 1], final[PG + 1 : PG + 2]], axis=1)
    finish(PG - 1)
    wholes = {
        "core small": s_core, "core": out_c, "far": out_f, "near": out_n, "small": r_p, "small z": r_z,
        "z": out_d.at[:, pl.ds(1, nz - 1)], "x": out_d.at[pl.ds(HOPS, PG - HOPS), 0, 0], "hop": out_h,
    }
    for departure in departures:
        departed(departure, wholes[departure])


def scale_kernel(norm_rows, all_rows, gram_in, rhs_in, tot_in, gram_ref, rhs_ref, tot_ref):
    gram_ref[...] = gram_in[...] / norm_rows
    rhs_ref[...] = rhs_in[...] / norm_rows
    rows = tot_in.shape[1] // 2
    tot_ref[0] = jnp.sum(tot_in[:, :rows]) / all_rows
    tot_ref[1] = jnp.sum(tot_in[:, rows:]) / all_rows


def fused(basis, residual, sigma, counts, pulsar, ecorr):
    ndp = lax.axis_size("dp")
    groups, slots, rows, width = basis.shape[1:]
    share = width // ndp
    nz = ndp // 2
    norm_rows = float(ndp * slots * rows)
    all_rows = float(ndp * groups * groups * slots * rows)
    vmem = pl.BlockSpec(memory_space=pltpu.VMEM)
    hw = width // 2
    tile = (2, 2 * PG, hw)
    n_arrivals = 2 + 3 + PG + 1 + 1 + PG + (PG - HOPS) + 1
    sums = pl.pallas_call(
        functools.partial(kernel, ndp),
        out_shape=(
            pltpu.VMEM((PG, share, width), F32),
            pltpu.VMEM((PG, share), F32),
            pltpu.VMEM((1, 2 * rows), F32),
        ),
        in_specs=[pl.BlockSpec(memory_space=pltpu.HBM)] * 6,
        out_specs=(vmem, vmem, vmem),
        scratch_shapes=[
            pltpu.VMEM((slots, rows, width), BF16),
            pltpu.VMEM((slots, rows, width), BF16),
            pltpu.VMEM((slots, rows, width), BF16),
            pltpu.VMEM((slots, rows, width), BF16),
            pltpu.VMEM((groups, slots, rows), BF16),
            pltpu.VMEM((groups, slots, rows), BF16),
            pltpu.VMEM((groups, slots), jnp.int32),
            pltpu.VMEM((groups, slots), jnp.int32),
            pltpu.VMEM((1, ecorr.shape[0]), F32),
            pltpu.SMEM((groups, slots), jnp.int32),
            *[pltpu.VMEM((slots + 1, 2, hw, hw), F32)] * groups,
            *[pltpu.VMEM((slots + 1, 8, hw), F32)] * groups,
            pltpu.VMEM((groups * slots, 8, rows), F32),
            *[pltpu.VMEM((slots, 8, width), F32)] * groups,
            pltpu.VMEM((2 * PG, 2, hw, hw), BF16),
            pltpu.VMEM((2 * PG, 2, hw, hw), BF16),
            pltpu.VMEM((PG, 2, hw, hw), BF16),
            pltpu.VMEM((PG, hw, hw), BF16),
            pltpu.VMEM((PG, 3, hw, hw), BF16),
            pltpu.VMEM((PG, nz, 2, share, hw), BF16),
            pltpu.VMEM((PG, nz, 2, share, hw), BF16),
            pltpu.VMEM((HOPS, 2, share, hw), F32),
            pltpu.VMEM((HOPS, share, hw), BF16),
            pltpu.VMEM((HOPS, share, hw), BF16),
            pltpu.VMEM((2,) + tile, F32),
            pltpu.VMEM((2,) + tile, F32),
            pltpu.VMEM(tile, F32),
            pltpu.VMEM(tile, F32),
            pltpu.VMEM((3,) + tile, F32),
            pltpu.VMEM(tile, F32),
            pltpu.VMEM((nz - 1,) + tile[1:], F32),
            pltpu.SemaphoreType.DMA((8,)),
            pltpu.SemaphoreType.DMA((9,)),
            pltpu.SemaphoreType.DMA((n_arrivals,)),
        ],
        compiler_params=pltpu.CompilerParams(
            collective_id=0, has_side_effects=True
        ),
    )(basis[0], residual[0], sigma[0], counts[0], pulsar[0], ecorr.reshape(1, -1))
    return pl.pallas_call(
        functools.partial(scale_kernel, norm_rows, all_rows),
        out_shape=(
            jax.ShapeDtypeStruct((PG, share, width), F32),
            jax.ShapeDtypeStruct((PG, share), F32),
            jax.ShapeDtypeStruct((2,), F32),
        ),
        in_specs=[vmem] * 3,
        out_specs=(vmem, vmem, pl.BlockSpec(memory_space=pltpu.SMEM)),
    )(*[pltpu.with_memory_space_constraint(a, pltpu.VMEM) for a in sums])


def slot_terms(basis, residual, sigma, counts, pulsar, group_ids, ecorr):
    sig = sigma.astype(jnp.float32)
    res = residual.astype(jnp.float32)
    rowpos = lax.broadcasted_iota(jnp.int32, sig.shape, 2)
    valid = rowpos < counts[..., None]
    inverse = jnp.where(valid, 1.0 / (sig * sig), jnp.float32(0.0))
    weighted = (inverse[..., None] * basis).astype(jnp.bfloat16)
    global_id = group_ids[:, None] * PG + pulsar
    table = jnp.arange(ecorr.shape[0], dtype=jnp.int32)
    chosen = jnp.sum(jnp.where(global_id[..., None] == table, ecorr, jnp.float32(0.0)), axis=-1)
    jitter = chosen * chosen
    total = jnp.sum(inverse, axis=2)
    coef = jitter / (1.0 + jitter * total)
    column = jnp.sum(weighted.astype(jnp.float32), axis=2)
    project = jnp.sum(weighted.astype(jnp.float32) * res[..., None], axis=2)
    wsum = jnp.sum(inverse * res, axis=2)
    chi = jnp.sum(inverse * res * res) - jnp.sum(coef * wsum * wsum)
    logdet = jnp.sum(jnp.where(valid, jnp.log(sig * sig), jnp.float32(0.0))) + jnp.sum(
        jnp.log(1.0 + jitter * total)
    )
    adjusted = project - (coef * wsum)[..., None] * column
    grams = []
    sums = []
    for member in range(PG):
        picked = pulsar == member
        masked = jnp.where(picked[..., None, None], weighted, jnp.zeros((), jnp.bfloat16))
        first = jnp.einsum("gslk,gslm->gkm", basis, masked, preferred_element_type=jnp.float32)
        scale = jnp.where(picked, coef, jnp.float32(0.0))
        minus = jnp.einsum(
            "gs,gsk,gsm->gkm", scale, column, column, precision=lax.Precision.HIGHEST
        )
        grams.append(first - minus)
        sums.append(jnp.sum(jnp.where(picked[..., None], adjusted, jnp.float32(0.0)), axis=1))
    return (jnp.stack(grams, axis=1), jnp.stack(sums, axis=1), logdet, chi)


def on_device(basis, residual, sigma, counts, pulsar, ecorr):
    groups = lax.axis_size("psr")
    ndp = lax.axis_size("dp")
    width = basis.shape[-1]
    rows = basis.shape[-2]
    slots = basis.shape[2]
    share = width // ndp
    group_ids = jnp.arange(groups, dtype=jnp.int32)
    gram, rhs, logdet, chi = slot_terms(
        basis[0], residual[0], sigma[0], counts[0], pulsar[0], group_ids, ecorr
    )
    gram_rows = (
        gram.reshape(groups, PG, ndp, share, width)
        .transpose(2, 0, 1, 3, 4)
        .reshape(ndp * groups * PG * share, width)
    )
    rhs_rows = (
        rhs.reshape(groups, PG, ndp, share).transpose(2, 0, 1, 3).reshape(ndp * groups * PG * share)
    )
    gram_part, rhs_part = (
        lax.psum_scatter(gram_rows, ("dp", "psr"), scatter_dimension=0, tiled=True),
        lax.psum_scatter(rhs_rows, ("dp", "psr"), scatter_dimension=0, tiled=True),
    )
    gram_part = gram_part.reshape(PG, share, width)
    rhs_part = rhs_part.reshape(PG, share)
    summed = lax.psum((logdet, chi), ("dp", "psr"))
    norm_rows = float(ndp * slots * rows)
    all_rows = float(ndp * groups * groups * slots * rows)
    totals = jnp.stack([summed[0], summed[1]]) / all_rows
    return (gram_part / norm_rows, rhs_part / norm_rows, totals)


def solution(mesh):
    def step(basis, *rest):
        groups, _, rows, width = basis.shape[1:]
        ndp = lax.axis_size("dp")
        tiled = ndp % 4 == 0 and width % (16 * ndp) == 0 and width % 256 == 0 and width == 2 * rows
        if groups == lax.axis_size("psr") == 2 * 2 and tiled:
            return fused(basis, *rest)
        return on_device(basis, *rest)

    return jax.shard_map(
        step,
        mesh=mesh,
        in_specs=(
            P(("dp", "psr"), None, None, None, None),
            P(("dp", "psr"), None, None, None),
            P(("dp", "psr"), None, None, None),
            P(("dp", "psr"), None, None),
            P(("dp", "psr"), None, None),
            P(),
        ),
        out_specs=(P("psr", "dp", None), P("psr", "dp"), P()),
        check_vma=False,
    )
```

```python
import functools

import jax
import jax.numpy as jnp
from jax import lax
from jax.experimental import pallas as pl
from jax.experimental.pallas import tpu as pltpu
from jax.sharding import PartitionSpec as P

PG = 4
HOPS = 2
MESH = pl.DeviceIdType.MESH
F32 = jnp.float32
BF16 = jnp.bfloat16


def stack_rows(ref, order):
    return jnp.concatenate([ref[g].astype(F32) for g in order], axis=0)


def columns(ref, order, slots):
    rows = [jnp.broadcast_to(ref[pl.ds(g, 1), :].astype(F32), (slots, slots)) for g in order]
    eye = jnp.concatenate([jnp.where(r == c, F32(1.0), F32(0.0)) for r, c in [triangle(slots)]] * len(order), axis=0)
    return jnp.sum(jnp.concatenate(rows, axis=0) * eye, axis=1, keepdims=True)


def slot_weights(order, res_ref, sig_ref, cnt_ref, pul_ref, ecorr_ref):
    slots, rows = sig_ref.shape[1:]
    n = len(order) * slots
    sig = stack_rows(sig_ref, order)
    res = stack_rows(res_ref, order)
    counts = columns(cnt_ref, order, slots)
    pulsar = columns(pul_ref, order, slots)
    base = jnp.concatenate([jnp.full((slots, 1), (g * PG).astype(F32)) for g in order], axis=0)
    lane = lax.broadcasted_iota(jnp.int32, (n, rows), 1)
    valid = lane.astype(F32) < counts
    var = sig * sig
    inverse = jnp.where(valid, 1.0 / var, F32(0.0))
    total = jnp.sum(inverse, axis=1, keepdims=True)
    n_table = ecorr_ref.shape[1]
    table = lax.broadcasted_iota(jnp.int32, (n, n_table), 1).astype(F32)
    chosen = jnp.sum(
        jnp.where(pulsar + base == table, jnp.broadcast_to(ecorr_ref[...], (n, n_table)), F32(0.0)),
        axis=1,
        keepdims=True,
    )
    jitter = chosen * chosen
    coef = jitter / (1.0 + jitter * total)
    wres = inverse * res
    wsum = jnp.sum(wres, axis=1, keepdims=True)
    first = lane == 0
    chi = wres * res - jnp.where(first, coef * wsum * wsum, F32(0.0))
    logdet = jnp.where(valid, jnp.log(var), F32(0.0)) + jnp.where(
        first, jnp.log(1.0 + jitter * total), F32(0.0)
    )
    tot = jnp.concatenate(
        [jnp.sum(logdet, axis=0, keepdims=True), jnp.sum(chi, axis=0, keepdims=True)], axis=1
    )
    return inverse, wres, coef, coef * wsum, pulsar, tot


def split(value):
    high = value.astype(BF16).astype(F32)
    return high, value - high


def group_left(inverse, wres, pulsar):
    slots, rows = inverse.shape
    slot = lax.broadcasted_iota(jnp.int32, (slots, rows), 0)
    member = lax.broadcasted_iota(jnp.int32, (PG, rows), 0).astype(F32)
    hots = [
        jnp.where(member == jnp.broadcast_to(pulsar[s : s + 1], (PG, rows)), F32(1.0), F32(0.0))
        for s in range(slots)
    ]

    def spread(a):
        return jnp.concatenate([jnp.where(slot == s, a, F32(0.0)) for s in range(slots)], axis=1)

    def hot(a):
        return jnp.concatenate([hots[s] * a[s : s + 1] for s in range(slots)], axis=1)

    left = [spread(a) for a in split(inverse)] + [hot(a) for a in split(wres)]
    return jnp.concatenate(left, axis=0).astype(BF16)


def group_sums(basis, inverse, wres, coef, cw, pulsar, shift_ref):
    slots, rows, width = basis.shape
    left = group_left(inverse, wres, pulsar)
    flat = basis[...].reshape(slots * rows, width)
    half = slots * rows // 2
    sums = jnp.dot(left[:, :half], flat[:half], preferred_element_type=F32) + jnp.dot(
        left[:, half:], flat[half:], preferred_element_type=F32
    )
    column = sums[:slots] + sums[slots : 2 * slots]
    project = sums[2 * slots : 2 * slots + PG] + sums[2 * slots + PG : 2 * slots + 2 * PG]
    minus = jnp.concatenate(
        [
            jnp.sum(jnp.where(pulsar == F32(m), cw, F32(0.0)) * column, axis=0, keepdims=True)
            for m in range(PG)
        ],
        axis=0,
    )
    shift = coef * column
    for s in range(slots):
        shift_ref[s] = jnp.broadcast_to(shift[s : s + 1], shift_ref.shape[1:])
    return project - minus


def slot_order(pulsars):
    rank = [jnp.int32(0)] * len(pulsars)
    for s in range(len(pulsars)):
        for t in range(s):
            before = jnp.where(pulsars[t] <= pulsars[s], 1, 0)
            rank[s] = rank[s] + before
            rank[t] = rank[t] + (1 - before)
    slots = range(len(pulsars))
    perm = [sum(jnp.where(rank[s] == j, s, 0) for s in slots) for j in slots]
    ends = [sum(jnp.where(p <= m, 1, 0) for p in pulsars) for m in range(PG - 1)]
    return perm, [0] + ends + [len(pulsars)]


def running_grams(basis, perm, first, inv_ref, shift_ref, run, run_diag):
    slots, rows, width = basis.shape
    hw = width // 2
    r, c = triangle(hw)
    for j in range(slots):
        s = perm[j]
        block = basis[s]
        centred = (block.astype(F32).reshape(rows // 8, 8, width) - shift_ref[s][None]).reshape(rows, width)
        weighted = (block.T.astype(F32).reshape(width // 8, 8, rows) * inv_ref[first + s][None]).reshape(width, rows)
        weighted, centred = weighted.astype(BF16), centred.astype(BF16)
        top = jnp.dot(weighted[:hw], centred, preferred_element_type=F32)
        low = jnp.dot(weighted[hw:], centred[:, hw:], preferred_element_type=F32)
        cross = top[:, hw:]
        both = jnp.where(r <= c, top[:, :hw], low)
        diag = jnp.broadcast_to(jnp.sum(jnp.where(r == c, low, F32(0.0)), axis=0, keepdims=True), (8, hw))
        if j:
            cross = cross + run[j, 0]
            both = both + run[j, 1]
            diag = diag + run_diag[j]
        run[j + 1, 0] = cross
        run[j + 1, 1] = both
        run_diag[j + 1] = diag


def triangle(n):
    return lax.broadcasted_iota(jnp.int32, (n, n), 0), lax.broadcasted_iota(jnp.int32, (n, n), 1)


def small_tiles(ref, rhs, diag, tot):
    hw = rhs.shape[1] // 2
    for h in range(2):
        rows = [rhs[:, h * hw : (h + 1) * hw], tot[:, :hw], tot[:, hw:]] + diag[h * PG // 2 : (h + 1) * PG // 2]
        ref[h] = jnp.concatenate(rows, axis=0)


def kernel(
    ndp,
    basis_ref, res_in, sig_in, cnt_in, pul_in, ecorr_in,
    gram_ref, rhs_ref, tot_ref,
    buf0, buf1, buf2, buf3, res_ref, sig_ref, cnt_ref, pul_ref, ecorr_ref, ids_ref,
    run0, run1, run2, run3, diag0, diag1, diag2, diag3, inv_ref, shift0, shift1, shift2, shift3,
    out_c, in_c, out_f, out_n, in_p, out_d, in_d, acc, out_h, in_h,
    s_core, r_core, s_near, s_far, r_p, s_z, r_z,
    load_sem, send_sem, recv_sem,
):
    nz = ndp // 2
    dp = lax.axis_index("dp")
    psr = lax.axis_index("psr")
    c, y = psr % 2, psr // 2
    x, z = dp % 2, dp // 2
    c2, y2, x2 = 1 - c, 1 - y, 1 - x
    core_peer = (dp, y * 2 + c2)
    y_peer = (dp, y2 * 2 + c)
    x_peer = (z * 2 + x2, psr)
    xy_peer = (z * 2 + x2, y2 * 2 + c)
    steps = [(k, j) for k in range(1, nz) for j in range(2)] + [(0, 1)]
    dp_peers = {(k, j): (((z + k) % nz) * 2 + (x + j) % 2, psr) for k, j in steps}
    order = (y2 * 2 + c2, y2 * 2 + c, y * 2 + c2, psr)
    bufs = (buf0, buf1, buf2, buf3)
    runs = (run0, run1, run2, run3)
    diags = (diag0, diag1, diag2, diag3)
    shifts = (shift0, shift1, shift2, shift3)

    barrier = pltpu.get_barrier_semaphore()
    greeted = list(dp_peers.values()) + [xy_peer, y_peer, core_peer]
    small_loads = []
    pairs = ((sig_in, sig_ref), (cnt_in, cnt_ref), (pul_in, ids_ref), (res_in, res_ref), (pul_in, pul_ref))
    for i, (src, dst) in enumerate(pairs + ((ecorr_in, ecorr_ref),)):
        load = pltpu.make_async_copy(src, dst, load_sem.at[2 + i])
        load.start()
        small_loads.append(load)
    loads = []
    for i, g in enumerate(order):
        load = pltpu.make_async_copy(basis_ref.at[g], bufs[i], load_sem.at[min(i, 1)])
        load.start()
        loads.append(load)

    for peer in greeted:
        pl.semaphore_signal(barrier, inc=1, device_id=peer, device_id_type=MESH)
    arrivals, departures = {}, {}

    def send(src, dst, peer, arrival, departure):
        copy = pltpu.make_async_remote_copy(
            src_ref=src, dst_ref=dst,
            send_sem=send_sem.at[departures.setdefault(departure, len(departures))],
            recv_sem=recv_sem.at[arrivals.setdefault(arrival, len(arrivals))],
            device_id=peer, device_id_type=MESH,
        )
        copy.start()

    def arrived(arrival, whole):
        pltpu.make_async_remote_copy(
            src_ref=whole, dst_ref=whole, send_sem=send_sem.at[0], recv_sem=recv_sem.at[arrivals[arrival]],
            device_id=core_peer, device_id_type=MESH,
        ).wait_recv()

    def departed(departure, whole):
        pltpu.make_async_remote_copy(
            src_ref=whole, dst_ref=whole, send_sem=send_sem.at[departures[departure]], recv_sem=recv_sem.at[0],
            device_id=core_peer, device_id_type=MESH,
        ).wait_send()

    for load in small_loads:
        load.wait()
    loads[0].wait()
    slots = sig_ref.shape[1]
    inverse, wres, coef, cw, pulsar, tot = slot_weights(order, res_ref, sig_ref, cnt_ref, pul_ref, ecorr_ref)

    for i in range(len(order) * slots):
        inv_ref[i] = jnp.broadcast_to(inverse[i : i + 1], inv_ref.shape[1:])
    for i in range(len(order)):
        runs[i][0] = jnp.zeros(runs[i].shape[1:], F32)
        diags[i][0] = jnp.zeros(diags[i].shape[1:], F32)
    rhs, ends = {}, {}

    def head(i):
        mine = slice(i * slots, (i + 1) * slots)
        rhs[i] = group_sums(
            bufs[i], inverse[mine], wres[mine], coef[mine], cw[mine], pulsar[mine], shifts[i]
        )

    def grams(i):
        perm, ends[i] = slot_order([ids_ref[order[i], s] for s in range(slots)])
        running_grams(bufs[i], perm, i * slots, inv_ref, shifts[i], runs[i], diags[i])

    def member(i, m, h):
        value = runs[i][ends[i][m + 1], h]
        return value - runs[i][ends[i][m], h] if m else value

    def small(ref, i):
        rows = [diags[i][e][:1] for e in ends[i]]
        small_tiles(ref, rhs[i], [rows[m + 1] - rows[m] for m in range(PG)], tot)

    def to_core(n, i):
        small(s_core.at[n], i)
        for m in range(PG):
            for h in range(2):
                out_c[n * PG + m, h] = member(i, m, h).astype(BF16)

    def core_sends(n):
        send(s_core.at[n], r_core.at[n], core_peer, ("core small", n), "tiles")
        for m in range(PG):
            key = "near" if n else ("far", min(m, 1))
            send(out_c.at[n * PG + m], in_c.at[n * PG + m], core_peer, key, "grams")

    head(0)
    grams(0)
    to_core(0, 0)
    pl.semaphore_wait(barrier, len(greeted))
    core_sends(0)
    rest = basis_ref.at[pl.ds(1, len(loads) - 1)]
    pltpu.make_async_copy(rest, rest, load_sem.at[1]).wait()
    head(1)
    head(2)
    head(3)
    grams(1)
    grams(2)
    to_core(1, 2)
    core_sends(1)
    small(s_far, 1)
    arrived(("core small", 0), r_core.at[0])
    s_far[...] = s_far[...] + r_core[0]
    send(s_far, r_p.at[0], y_peer, "small", "tiles")
    send(s_far, r_p.at[1], xy_peer, "small", "tiles")
    def far_sum(m):
        if m == 0:
            arrived(("far", 0), in_c.at[0])
        if m == 1:
            arrived(("far", 1), in_c.at[pl.ds(1, PG - 1)])
        for h in range(2):
            out_f[m, h] = (member(1, m, h) + in_c[m, h].astype(F32)).astype(BF16)

    def to_y(m):
        send(out_f.at[m, x], in_p.at[m, 0], y_peer, ("plane", m), "grams")

    def to_xy(m):
        send(out_f.at[m, x2], in_p.at[m, 1], xy_peer, ("plane", m), "grams")

    def to_x(m):
        out_n[m] = (member(3, m, x2) + in_c[PG + m, x2].astype(F32)).astype(BF16)
        send(out_n.at[m], in_p.at[m, 2], x_peer, ("plane", m), "grams")

    far_sum(0)
    to_y(0)
    to_xy(0)
    far_sum(1)
    to_y(1)
    far_sum(2)
    to_y(2)
    far_sum(3)
    to_y(3)
    grams(3)
    small(s_near, 3)
    arrived(("core small", 1), r_core.at[1])
    arrived("near", in_c.at[pl.ds(PG, PG)])
    s_near[...] = s_near[...] + r_core[1]
    send(s_near, r_p.at[2], x_peer, "small", "tiles")
    to_x(0)
    to_xy(1)
    to_x(1)
    to_xy(2)
    to_x(2)
    to_xy(3)
    to_x(3)

    total = s_near[...]
    arrived("small", r_p)
    for i in range(3):
        total = total + r_p[i]
    s_z[...] = total
    hz = nz // 2
    for k in range(1, nz):
        send(s_z.at[((z + k) % nz) // hz], r_z.at[k - 1], dp_peers[k, 0], "small z", "tiles")

    hw = out_n.shape[1]
    row, col = triangle(hw)
    crossed = x == 0
    upper = jnp.logical_or(row <= col, crossed)
    lower = jnp.logical_and(row > col, jnp.logical_not(crossed))
    middle = jnp.logical_and(row == col, jnp.logical_not(crossed))

    def to_all(m):
        value = member(3, m, x) + in_c[PG + m, x].astype(F32)
        arrived(("plane", m), in_p.at[m])
        for i in range(3):
            value = value + in_p[m, i].astype(F32)
        value = value.astype(BF16)
        turned = value.T.astype(F32)
        value = value.astype(F32)
        at = PG + 2 + m % (PG // 2)
        diag = jnp.broadcast_to(total[m // (PG // 2), at : at + 1], (hw, hw))
        top = jnp.where(upper, value, turned)
        low = jnp.where(lower, value, jnp.where(middle, diag, turned))
        out_d[m] = jnp.concatenate([top, low], axis=0).astype(BF16).reshape(out_d.shape[1:])
        for k in range(1, nz):
            if m < HOPS:
                send(out_d.at[m, (z + k) % nz], in_d.at[m, k], dp_peers[k, 0], ("z", m), "z")
        if m >= HOPS:
            for k, j in steps:
                keys = (("z", m), "z") if k else (("x", m), "x")
                send(out_d.at[m, (z + k) % nz, (x + j) % 2], in_d.at[m, k, j], dp_peers[k, j], *keys)

    def hop(m):
        both = out_d[m, z].astype(F32)
        arrived(("z", m), in_d.at[m, pl.ds(1, nz - 1)])
        for k in range(1, nz):
            both = both + in_d[m, k].astype(F32)
        acc[m] = both
        out_h[m] = acc[m, x2].astype(BF16)
        send(out_h.at[m], in_h.at[m], x_peer, "hop", "hop")

    def finish(m):
        if m < HOPS:
            if m == 0:
                arrived("hop", in_h)
            own = acc[m, x]
            other = in_h[m].astype(F32)
        else:
            own = out_d[m, z, x].astype(F32)
            arrived(("x", m), in_d.at[m, 0, 1])
            arrived(("z", m), in_d.at[m, pl.ds(1, nz - 1)])
            for k in range(1, nz):
                own = own + in_d[m, k, 0].astype(F32)
            other = in_d[m, 0, 1].astype(F32)
            for k in range(1, nz):
                other = other + in_d[m, k, 1].astype(F32)
        swap = (x + z // hz) % 2 == 0
        left = jnp.where(swap, other, own)
        gram_ref[m] = jnp.concatenate([left, jnp.where(swap, own, other)], axis=1)

    for m in range(PG):
        to_all(m)
    for m in range(HOPS):
        hop(m)
    for m in range(PG - 1):
        finish(m)
    final = s_z[z // hz]
    arrived("small z", r_z)
    for k in range(1, nz):
        final = final + r_z[k - 1]
    share = rhs_ref.shape[1]
    mine = jnp.zeros((PG, share), F32)
    for e in range(hw // share):
        mine = mine + jnp.where(dp % (hw // share) == e, final[:PG, e * share : (e + 1) * share], F32(0.0))
    rhs_ref[...] = mine
    tot_ref[...] = jnp.concatenate([final[PG : PG + 1], final[PG + 1 : PG + 2]], axis=1)
    finish(PG - 1)
    wholes = {
        "grams": run0.at[pl.ds(0, 7 * PG // 4)], "tiles": inv_ref.at[pl.ds(0, 10 + nz - 1)],
        "z": out_d.at[:, pl.ds(1, nz - 1)], "x": out_d.at[pl.ds(HOPS, PG - HOPS), 0, 0], "hop": out_h,
    }
    for departure in departures:
        departed(departure, wholes[departure])


def scale_kernel(norm_rows, all_rows, gram_in, rhs_in, tot_in, gram_ref, rhs_ref, tot_ref):
    gram_ref[...] = gram_in[...] / norm_rows
    rhs_ref[...] = rhs_in[...] / norm_rows
    rows = tot_in.shape[1] // 2
    tot_ref[0] = jnp.sum(tot_in[:, :rows]) / all_rows
    tot_ref[1] = jnp.sum(tot_in[:, rows:]) / all_rows


def fused(basis, residual, sigma, counts, pulsar, ecorr):
    ndp = lax.axis_size("dp")
    groups, slots, rows, width = basis.shape[1:]
    share = width // ndp
    nz = ndp // 2
    norm_rows = float(ndp * slots * rows)
    all_rows = float(ndp * groups * groups * slots * rows)
    vmem = pl.BlockSpec(memory_space=pltpu.VMEM)
    hw = width // 2
    tile = (2, 2 * PG, hw)
    n_arrivals = 2 + 3 + PG + 1 + 1 + PG + (PG - HOPS) + 1
    sums = pl.pallas_call(
        functools.partial(kernel, ndp),
        out_shape=(
            pltpu.VMEM((PG, share, width), F32),
            pltpu.VMEM((PG, share), F32),
            pltpu.VMEM((1, 2 * rows), F32),
        ),
        in_specs=[pl.BlockSpec(memory_space=pltpu.HBM)] * 6,
        out_specs=(vmem, vmem, vmem),
        scratch_shapes=[
            pltpu.VMEM((slots, rows, width), BF16),
            pltpu.VMEM((slots, rows, width), BF16),
            pltpu.VMEM((slots, rows, width), BF16),
            pltpu.VMEM((slots, rows, width), BF16),
            pltpu.VMEM((groups, slots, rows), BF16),
            pltpu.VMEM((groups, slots, rows), BF16),
            pltpu.VMEM((groups, slots), jnp.int32),
            pltpu.VMEM((groups, slots), jnp.int32),
            pltpu.VMEM((1, ecorr.shape[0]), F32),
            pltpu.SMEM((groups, slots), jnp.int32),
            *[pltpu.VMEM((slots + 1, 2, hw, hw), F32)] * groups,
            *[pltpu.VMEM((slots + 1, 8, hw), F32)] * groups,
            pltpu.VMEM((groups * slots, 8, rows), F32),
            *[pltpu.VMEM((slots, 8, width), F32)] * groups,
            pltpu.VMEM((2 * PG, 2, hw, hw), BF16),
            pltpu.VMEM((2 * PG, 2, hw, hw), BF16),
            pltpu.VMEM((PG, 2, hw, hw), BF16),
            pltpu.VMEM((PG, hw, hw), BF16),
            pltpu.VMEM((PG, 3, hw, hw), BF16),
            pltpu.VMEM((PG, nz, 2, share, hw), BF16),
            pltpu.VMEM((PG, nz, 2, share, hw), BF16),
            pltpu.VMEM((HOPS, 2, share, hw), F32),
            pltpu.VMEM((HOPS, share, hw), BF16),
            pltpu.VMEM((HOPS, share, hw), BF16),
            pltpu.VMEM((2,) + tile, F32),
            pltpu.VMEM((2,) + tile, F32),
            pltpu.VMEM(tile, F32),
            pltpu.VMEM(tile, F32),
            pltpu.VMEM((3,) + tile, F32),
            pltpu.VMEM(tile, F32),
            pltpu.VMEM((nz - 1,) + tile[1:], F32),
            pltpu.SemaphoreType.DMA((8,)),
            pltpu.SemaphoreType.DMA((5,)),
            pltpu.SemaphoreType.DMA((n_arrivals,)),
        ],
        compiler_params=pltpu.CompilerParams(
            collective_id=0, has_side_effects=True
        ),
    )(basis[0], residual[0], sigma[0], counts[0], pulsar[0], ecorr.reshape(1, -1))
    return pl.pallas_call(
        functools.partial(scale_kernel, norm_rows, all_rows),
        out_shape=(
            jax.ShapeDtypeStruct((PG, share, width), F32),
            jax.ShapeDtypeStruct((PG, share), F32),
            jax.ShapeDtypeStruct((2,), F32),
        ),
        in_specs=[vmem] * 3,
        out_specs=(vmem, vmem, pl.BlockSpec(memory_space=pltpu.SMEM)),
    )(*[pltpu.with_memory_space_constraint(a, pltpu.VMEM) for a in sums])


def slot_terms(basis, residual, sigma, counts, pulsar, group_ids, ecorr):
    sig = sigma.astype(jnp.float32)
    res = residual.astype(jnp.float32)
    rowpos = lax.broadcasted_iota(jnp.int32, sig.shape, 2)
    valid = rowpos < counts[..., None]
    inverse = jnp.where(valid, 1.0 / (sig * sig), jnp.float32(0.0))
    weighted = (inverse[..., None] * basis).astype(jnp.bfloat16)
    global_id = group_ids[:, None] * PG + pulsar
    table = jnp.arange(ecorr.shape[0], dtype=jnp.int32)
    chosen = jnp.sum(jnp.where(global_id[..., None] == table, ecorr, jnp.float32(0.0)), axis=-1)
    jitter = chosen * chosen
    total = jnp.sum(inverse, axis=2)
    coef = jitter / (1.0 + jitter * total)
    column = jnp.sum(weighted.astype(jnp.float32), axis=2)
    project = jnp.sum(weighted.astype(jnp.float32) * res[..., None], axis=2)
    wsum = jnp.sum(inverse * res, axis=2)
    chi = jnp.sum(inverse * res * res) - jnp.sum(coef * wsum * wsum)
    logdet = jnp.sum(jnp.where(valid, jnp.log(sig * sig), jnp.float32(0.0))) + jnp.sum(
        jnp.log(1.0 + jitter * total)
    )
    adjusted = project - (coef * wsum)[..., None] * column
    grams = []
    sums = []
    for member in range(PG):
        picked = pulsar == member
        masked = jnp.where(picked[..., None, None], weighted, jnp.zeros((), jnp.bfloat16))
        first = jnp.einsum("gslk,gslm->gkm", basis, masked, preferred_element_type=jnp.float32)
        scale = jnp.where(picked, coef, jnp.float32(0.0))
        minus = jnp.einsum(
            "gs,gsk,gsm->gkm", scale, column, column, precision=lax.Precision.HIGHEST
        )
        grams.append(first - minus)
        sums.append(jnp.sum(jnp.where(picked[..., None], adjusted, jnp.float32(0.0)), axis=1))
    return (jnp.stack(grams, axis=1), jnp.stack(sums, axis=1), logdet, chi)


def on_device(basis, residual, sigma, counts, pulsar, ecorr):
    groups = lax.axis_size("psr")
    ndp = lax.axis_size("dp")
    width = basis.shape[-1]
    rows = basis.shape[-2]
    slots = basis.shape[2]
    share = width // ndp
    group_ids = jnp.arange(groups, dtype=jnp.int32)
    gram, rhs, logdet, chi = slot_terms(
        basis[0], residual[0], sigma[0], counts[0], pulsar[0], group_ids, ecorr
    )
    gram_rows = (
        gram.reshape(groups, PG, ndp, share, width)
        .transpose(2, 0, 1, 3, 4)
        .reshape(ndp * groups * PG * share, width)
    )
    rhs_rows = (
        rhs.reshape(groups, PG, ndp, share).transpose(2, 0, 1, 3).reshape(ndp * groups * PG * share)
    )
    gram_part, rhs_part = (
        lax.psum_scatter(gram_rows, ("dp", "psr"), scatter_dimension=0, tiled=True),
        lax.psum_scatter(rhs_rows, ("dp", "psr"), scatter_dimension=0, tiled=True),
    )
    gram_part = gram_part.reshape(PG, share, width)
    rhs_part = rhs_part.reshape(PG, share)
    summed = lax.psum((logdet, chi), ("dp", "psr"))
    norm_rows = float(ndp * slots * rows)
    all_rows = float(ndp * groups * groups * slots * rows)
    totals = jnp.stack([summed[0], summed[1]]) / all_rows
    return (gram_part / norm_rows, rhs_part / norm_rows, totals)


def solution(mesh):
    def step(basis, *rest):
        groups, _, rows, width = basis.shape[1:]
        ndp = lax.axis_size("dp")
        tiled = ndp % 4 == 0 and width % (16 * ndp) == 0 and width % 256 == 0 and width == 2 * rows
        if groups == lax.axis_size("psr") == 2 * 2 and tiled:
            return fused(basis, *rest)
        return on_device(basis, *rest)

    return jax.shard_map(
        step,
        mesh=mesh,
        in_specs=(
            P(("dp", "psr"), None, None, None, None),
            P(("dp", "psr"), None, None, None),
            P(("dp", "psr"), None, None, None),
            P(("dp", "psr"), None, None),
            P(("dp", "psr"), None, None),
            P(),
        ),
        out_specs=(P("psr", "dp", None), P("psr", "dp"), P()),
        check_vma=False,
    )
```

```python
import functools

import jax
import jax.numpy as jnp
from jax import lax
from jax.experimental import pallas as pl
from jax.experimental.pallas import tpu as pltpu
from jax.sharding import PartitionSpec as P

PG = 4
HOPS = 1
MESH = pl.DeviceIdType.MESH
F32 = jnp.float32
BF16 = jnp.bfloat16


def stack_rows(ref, order):
    return jnp.concatenate([ref[g].astype(F32) for g in order], axis=0)


def columns(ref, order, slots):
    rows = [jnp.broadcast_to(ref[pl.ds(g, 1), :].astype(F32), (slots, slots)) for g in order]
    eye = jnp.concatenate([jnp.where(r == c, F32(1.0), F32(0.0)) for r, c in [triangle(slots)]] * len(order), axis=0)
    return jnp.sum(jnp.concatenate(rows, axis=0) * eye, axis=1, keepdims=True)


def slot_weights(order, res_ref, sig_ref, cnt_ref, pul_ref, ecorr_ref):
    slots, rows = sig_ref.shape[1:]
    n = len(order) * slots
    sig = stack_rows(sig_ref, order)
    res = stack_rows(res_ref, order)
    counts = columns(cnt_ref, order, slots)
    pulsar = columns(pul_ref, order, slots)
    base = jnp.concatenate([jnp.full((slots, 1), (g * PG).astype(F32)) for g in order], axis=0)
    lane = lax.broadcasted_iota(jnp.int32, (n, rows), 1)
    valid = lane.astype(F32) < counts
    var = sig * sig
    inverse = jnp.where(valid, 1.0 / var, F32(0.0))
    total = jnp.sum(inverse, axis=1, keepdims=True)
    n_table = ecorr_ref.shape[1]
    table = lax.broadcasted_iota(jnp.int32, (n, n_table), 1).astype(F32)
    chosen = jnp.sum(
        jnp.where(pulsar + base == table, jnp.broadcast_to(ecorr_ref[...], (n, n_table)), F32(0.0)),
        axis=1,
        keepdims=True,
    )
    jitter = chosen * chosen
    coef = jitter / (1.0 + jitter * total)
    wres = inverse * res
    wsum = jnp.sum(wres, axis=1, keepdims=True)
    first = lane == 0
    chi = wres * res - jnp.where(first, coef * wsum * wsum, F32(0.0))
    logdet = jnp.where(valid, jnp.log(var), F32(0.0)) + jnp.where(
        first, jnp.log(1.0 + jitter * total), F32(0.0)
    )
    tot = jnp.concatenate(
        [jnp.sum(logdet, axis=0, keepdims=True), jnp.sum(chi, axis=0, keepdims=True)], axis=1
    )
    return inverse, wres, coef, coef * wsum, pulsar, tot


def split(value):
    high = value.astype(BF16).astype(F32)
    return high, value - high


def group_left(inverse, wres, pulsar):
    slots, rows = inverse.shape
    slot = lax.broadcasted_iota(jnp.int32, (slots, rows), 0)
    member = lax.broadcasted_iota(jnp.int32, (PG, rows), 0).astype(F32)
    hots = [
        jnp.where(member == jnp.broadcast_to(pulsar[s : s + 1], (PG, rows)), F32(1.0), F32(0.0))
        for s in range(slots)
    ]

    def spread(a):
        return jnp.concatenate([jnp.where(slot == s, a, F32(0.0)) for s in range(slots)], axis=1)

    def hot(a):
        return jnp.concatenate([hots[s] * a[s : s + 1] for s in range(slots)], axis=1)

    left = [spread(a) for a in split(inverse)] + [hot(a) for a in split(wres)]
    return jnp.concatenate(left, axis=0).astype(BF16)


def group_sums(basis, inverse, wres, coef, cw, pulsar, shift_ref):
    slots, rows, width = basis.shape
    left = group_left(inverse, wres, pulsar)
    flat = basis[...].reshape(slots * rows, width)
    half = slots * rows // 2
    sums = jnp.dot(left[:, :half], flat[:half], preferred_element_type=F32) + jnp.dot(
        left[:, half:], flat[half:], preferred_element_type=F32
    )
    column = sums[:slots] + sums[slots : 2 * slots]
    project = sums[2 * slots : 2 * slots + PG] + sums[2 * slots + PG : 2 * slots + 2 * PG]
    minus = jnp.concatenate(
        [
            jnp.sum(jnp.where(pulsar == F32(m), cw, F32(0.0)) * column, axis=0, keepdims=True)
            for m in range(PG)
        ],
        axis=0,
    )
    shift = coef * column
    for s in range(slots):
        shift_ref[s] = jnp.broadcast_to(shift[s : s + 1], shift_ref.shape[1:])
    return project - minus


def slot_order(pulsars):
    rank = [jnp.int32(0)] * len(pulsars)
    for s in range(len(pulsars)):
        for t in range(s):
            before = jnp.where(pulsars[t] <= pulsars[s], 1, 0)
            rank[s] = rank[s] + before
            rank[t] = rank[t] + (1 - before)
    slots = range(len(pulsars))
    perm = [sum(jnp.where(rank[s] == j, s, 0) for s in slots) for j in slots]
    ends = [sum(jnp.where(p <= m, 1, 0) for p in pulsars) for m in range(PG - 1)]
    return perm, [0] + ends + [len(pulsars)]


def running_grams(basis, perm, first, inv_ref, shift_ref, run, run_diag):
    slots, rows, width = basis.shape
    hw = width // 2
    r, c = triangle(hw)
    for j in range(slots):
        s = perm[j]
        block = basis[s]
        centred = (block.astype(F32).reshape(rows // 8, 8, width) - shift_ref[s][None]).reshape(rows, width)
        weighted = (block.T.astype(F32).reshape(width // 8, 8, rows) * inv_ref[first + s][None]).reshape(width, rows)
        weighted, centred = weighted.astype(BF16), centred.astype(BF16)
        top = jnp.dot(weighted[:hw], centred, preferred_element_type=F32)
        low = jnp.dot(weighted[hw:], centred[:, hw:], preferred_element_type=F32)
        cross = top[:, hw:]
        both = jnp.where(r <= c, top[:, :hw], low)
        diag = jnp.broadcast_to(jnp.sum(jnp.where(r == c, low, F32(0.0)), axis=0, keepdims=True), (8, hw))
        if j:
            cross = cross + run[j, 0]
            both = both + run[j, 1]
            diag = diag + run_diag[j]
        run[j + 1, 0] = cross
        run[j + 1, 1] = both
        run_diag[j + 1] = diag


def triangle(n):
    return lax.broadcasted_iota(jnp.int32, (n, n), 0), lax.broadcasted_iota(jnp.int32, (n, n), 1)


def small_tiles(ref, rhs, diag, tot):
    hw = rhs.shape[1] // 2
    for h in range(2):
        rows = [rhs[:, h * hw : (h + 1) * hw], tot[:, :hw], tot[:, hw:]] + diag[h * PG // 2 : (h + 1) * PG // 2]
        ref[h] = jnp.concatenate(rows, axis=0)


def kernel(
    ndp,
    basis_ref, res_in, sig_in, cnt_in, pul_in, ecorr_in,
    gram_ref, rhs_ref, tot_ref,
    buf0, buf1, buf2, buf3, res_ref, sig_ref, cnt_ref, pul_ref, ecorr_ref, ids_ref,
    run0, run1, run2, run3, diag0, diag1, diag2, diag3, inv_ref, shift0, shift1, shift2, shift3,
    out_c, in_c, out_f, out_n, in_p, out_d, in_d, acc, out_h, in_h,
    s_core, r_core, s_near, s_far, r_p, s_z, r_z,
    load_sem, send_sem, recv_sem,
):
    nz = ndp // 2
    dp = lax.axis_index("dp")
    psr = lax.axis_index("psr")
    c, y = psr % 2, psr // 2
    x, z = dp % 2, dp // 2
    c2, y2, x2 = 1 - c, 1 - y, 1 - x
    core_peer = (dp, y * 2 + c2)
    y_peer = (dp, y2 * 2 + c)
    x_peer = (z * 2 + x2, psr)
    xy_peer = (z * 2 + x2, y2 * 2 + c)
    steps = [(k, j) for k in range(1, nz) for j in range(2)] + [(0, 1)]
    dp_peers = {(k, j): (((z + k) % nz) * 2 + (x + j) % 2, psr) for k, j in steps}
    order = (y2 * 2 + c2, y2 * 2 + c, y * 2 + c2, psr)
    bufs = (buf0, buf1, buf2, buf3)
    runs = (run0, run1, run2, run3)
    diags = (diag0, diag1, diag2, diag3)
    shifts = (shift0, shift1, shift2, shift3)

    barrier = pltpu.get_barrier_semaphore()
    greeted = list(dp_peers.values()) + [xy_peer, y_peer, core_peer]
    small_loads = []
    pairs = ((sig_in, sig_ref), (cnt_in, cnt_ref), (pul_in, ids_ref), (res_in, res_ref), (pul_in, pul_ref))
    for i, (src, dst) in enumerate(pairs + ((ecorr_in, ecorr_ref),)):
        load = pltpu.make_async_copy(src, dst, load_sem.at[2 + i])
        load.start()
        small_loads.append(load)
    loads = []
    for i, g in enumerate(order):
        load = pltpu.make_async_copy(basis_ref.at[g], bufs[i], load_sem.at[min(i, 1)])
        load.start()
        loads.append(load)

    for peer in greeted:
        pl.semaphore_signal(barrier, inc=1, device_id=peer, device_id_type=MESH)
    arrivals, departures = {}, {}

    def send(src, dst, peer, arrival, departure):
        copy = pltpu.make_async_remote_copy(
            src_ref=src, dst_ref=dst,
            send_sem=send_sem.at[departures.setdefault(departure, len(departures))],
            recv_sem=recv_sem.at[arrivals.setdefault(arrival, len(arrivals))],
            device_id=peer, device_id_type=MESH,
        )
        copy.start()

    def arrived(arrival, whole):
        pltpu.make_async_remote_copy(
            src_ref=whole, dst_ref=whole, send_sem=send_sem.at[0], recv_sem=recv_sem.at[arrivals[arrival]],
            device_id=core_peer, device_id_type=MESH,
        ).wait_recv()

    def departed(departure, whole):
        pltpu.make_async_remote_copy(
            src_ref=whole, dst_ref=whole, send_sem=send_sem.at[departures[departure]], recv_sem=recv_sem.at[0],
            device_id=core_peer, device_id_type=MESH,
        ).wait_send()

    for load in small_loads:
        load.wait()
    loads[0].wait()
    slots = sig_ref.shape[1]
    inverse, wres, coef, cw, pulsar, tot = slot_weights(order, res_ref, sig_ref, cnt_ref, pul_ref, ecorr_ref)

    for i in range(len(order) * slots):
        inv_ref[i] = jnp.broadcast_to(inverse[i : i + 1], inv_ref.shape[1:])
    for i in range(len(order)):
        runs[i][0] = jnp.zeros(runs[i].shape[1:], F32)
        diags[i][0] = jnp.zeros(diags[i].shape[1:], F32)
    rhs, ends = {}, {}

    def head(i):
        mine = slice(i * slots, (i + 1) * slots)
        rhs[i] = group_sums(
            bufs[i], inverse[mine], wres[mine], coef[mine], cw[mine], pulsar[mine], shifts[i]
        )

    def grams(i):
        perm, ends[i] = slot_order([ids_ref[order[i], s] for s in range(slots)])
        running_grams(bufs[i], perm, i * slots, inv_ref, shifts[i], runs[i], diags[i])

    def member(i, m, h):
        value = runs[i][ends[i][m + 1], h]
        return value - runs[i][ends[i][m], h] if m else value

    def small(ref, i):
        rows = [diags[i][e][:1] for e in ends[i]]
        small_tiles(ref, rhs[i], [rows[m + 1] - rows[m] for m in range(PG)], tot)

    def to_core(n, i):
        small(s_core.at[n], i)
        for m in range(PG):
            for h in range(2):
                out_c[n * PG + m, h] = member(i, m, h).astype(BF16)

    def core_sends(n):
        send(s_core.at[n], r_core.at[n], core_peer, ("core small", n), "tiles")
        for m in range(PG):
            key = "near" if n else ("far", min(m, 1))
            send(out_c.at[n * PG + m], in_c.at[n * PG + m], core_peer, key, "grams")

    head(0)
    grams(0)
    to_core(0, 0)
    pl.semaphore_wait(barrier, len(greeted))
    core_sends(0)
    rest = basis_ref.at[pl.ds(1, len(loads) - 1)]
    pltpu.make_async_copy(rest, rest, load_sem.at[1]).wait()
    head(1)
    head(2)
    head(3)
    grams(1)
    grams(2)
    to_core(1, 2)
    core_sends(1)
    small(s_far, 1)
    arrived(("core small", 0), r_core.at[0])
    s_far[...] = s_far[...] + r_core[0]
    send(s_far, r_p.at[0], y_peer, "small", "tiles")
    send(s_far, r_p.at[1], xy_peer, "small", "tiles")
    def far_sum(m):
        if m == 0:
            arrived(("far", 0), in_c.at[0])
        if m == 1:
            arrived(("far", 1), in_c.at[pl.ds(1, PG - 1)])
        for h in range(2):
            out_f[m, h] = (member(1, m, h) + in_c[m, h].astype(F32)).astype(BF16)

    def to_y(m):
        send(out_f.at[m, x], in_p.at[m, 0], y_peer, ("plane", m), "grams")

    def to_xy(m):
        send(out_f.at[m, x2], in_p.at[m, 1], xy_peer, ("plane", m), "grams")

    def to_x(m):
        out_n[m] = (member(3, m, x2) + in_c[PG + m, x2].astype(F32)).astype(BF16)
        send(out_n.at[m], in_p.at[m, 2], x_peer, ("plane", m), "grams")

    far_sum(0)
    to_y(0)
    to_xy(0)
    far_sum(1)
    to_y(1)
    far_sum(2)
    to_y(2)
    far_sum(3)
    to_y(3)
    grams(3)
    small(s_near, 3)
    arrived(("core small", 1), r_core.at[1])
    arrived("near", in_c.at[pl.ds(PG, PG)])
    s_near[...] = s_near[...] + r_core[1]
    send(s_near, r_p.at[2], x_peer, "small", "tiles")
    to_x(0)
    to_xy(1)
    to_x(1)
    to_xy(2)
    to_x(2)
    to_xy(3)
    to_x(3)

    total = s_near[...]
    arrived("small", r_p)
    for i in range(3):
        total = total + r_p[i]
    s_z[...] = total
    hz = nz // 2
    for k in range(1, nz):
        send(s_z.at[((z + k) % nz) // hz], r_z.at[k - 1], dp_peers[k, 0], "small z", "tiles")

    hw = out_n.shape[1]
    row, col = triangle(hw)
    crossed = x == 0
    upper = jnp.logical_or(row <= col, crossed)
    lower = jnp.logical_and(row > col, jnp.logical_not(crossed))
    middle = jnp.logical_and(row == col, jnp.logical_not(crossed))

    def to_all(m):
        value = member(3, m, x) + in_c[PG + m, x].astype(F32)
        arrived(("plane", m), in_p.at[m])
        for i in range(3):
            value = value + in_p[m, i].astype(F32)
        value = value.astype(BF16)
        turned = value.T.astype(F32)
        value = value.astype(F32)
        at = PG + 2 + m % (PG // 2)
        diag = jnp.broadcast_to(total[m // (PG // 2), at : at + 1], (hw, hw))
        top = jnp.where(upper, value, turned)
        low = jnp.where(lower, value, jnp.where(middle, diag, turned))
        out_d[m] = jnp.concatenate([top, low], axis=0).astype(BF16).reshape(out_d.shape[1:])
        for k in range(1, nz):
            if m < HOPS:
                send(out_d.at[m, (z + k) % nz], in_d.at[m, k], dp_peers[k, 0], ("z", m), "z")
        if m >= HOPS:
            for k, j in steps:
                keys = (("z", m), "z") if k else (("x", m), "x")
                send(out_d.at[m, (z + k) % nz, (x + j) % 2], in_d.at[m, k, j], dp_peers[k, j], *keys)

    def hop(m):
        both = out_d[m, z].astype(F32)
        arrived(("z", m), in_d.at[m, pl.ds(1, nz - 1)])
        for k in range(1, nz):
            both = both + in_d[m, k].astype(F32)
        acc[m] = both
        out_h[m] = acc[m, x2].astype(BF16)
        send(out_h.at[m], in_h.at[m], x_peer, "hop", "hop")

    def finish(m):
        if m < HOPS:
            if m == 0:
                arrived("hop", in_h)
            own = acc[m, x]
            other = in_h[m].astype(F32)
        else:
            own = out_d[m, z, x].astype(F32)
            arrived(("x", m), in_d.at[m, 0, 1])
            arrived(("z", m), in_d.at[m, pl.ds(1, nz - 1)])
            for k in range(1, nz):
                own = own + in_d[m, k, 0].astype(F32)
            other = in_d[m, 0, 1].astype(F32)
            for k in range(1, nz):
                other = other + in_d[m, k, 1].astype(F32)
        swap = (x + z // hz) % 2 == 0
        left = jnp.where(swap, other, own)
        gram_ref[m] = jnp.concatenate([left, jnp.where(swap, own, other)], axis=1)

    for m in range(PG):
        to_all(m)
    for m in range(HOPS):
        hop(m)
    for m in range(PG - 1):
        finish(m)
    final = s_z[z // hz]
    arrived("small z", r_z)
    for k in range(1, nz):
        final = final + r_z[k - 1]
    share = rhs_ref.shape[1]
    mine = jnp.zeros((PG, share), F32)
    for e in range(hw // share):
        mine = mine + jnp.where(dp % (hw // share) == e, final[:PG, e * share : (e + 1) * share], F32(0.0))
    rhs_ref[...] = mine
    tot_ref[...] = jnp.concatenate([final[PG : PG + 1], final[PG + 1 : PG + 2]], axis=1)
    finish(PG - 1)
    wholes = {
        "grams": run0.at[pl.ds(0, 7 * PG // 4)], "tiles": inv_ref.at[pl.ds(0, 10 + nz - 1)],
        "z": out_d.at[:, pl.ds(1, nz - 1)], "x": out_d.at[pl.ds(HOPS, PG - HOPS), 0, 0], "hop": out_h,
    }
    for departure in departures:
        departed(departure, wholes[departure])


def scale_kernel(norm_rows, all_rows, gram_in, rhs_in, tot_in, gram_ref, rhs_ref, tot_ref):
    gram_ref[...] = gram_in[...] / norm_rows
    rhs_ref[...] = rhs_in[...] / norm_rows
    rows = tot_in.shape[1] // 2
    tot_ref[0] = jnp.sum(tot_in[:, :rows]) / all_rows
    tot_ref[1] = jnp.sum(tot_in[:, rows:]) / all_rows


def fused(basis, residual, sigma, counts, pulsar, ecorr):
    ndp = lax.axis_size("dp")
    groups, slots, rows, width = basis.shape[1:]
    share = width // ndp
    nz = ndp // 2
    norm_rows = float(ndp * slots * rows)
    all_rows = float(ndp * groups * groups * slots * rows)
    vmem = pl.BlockSpec(memory_space=pltpu.VMEM)
    hw = width // 2
    tile = (2, 2 * PG, hw)
    n_arrivals = 2 + 3 + PG + 1 + 1 + PG + (PG - HOPS) + 1
    sums = pl.pallas_call(
        functools.partial(kernel, ndp),
        out_shape=(
            pltpu.VMEM((PG, share, width), F32),
            pltpu.VMEM((PG, share), F32),
            pltpu.VMEM((1, 2 * rows), F32),
        ),
        in_specs=[pl.BlockSpec(memory_space=pltpu.HBM)] * 6,
        out_specs=(vmem, vmem, vmem),
        scratch_shapes=[
            pltpu.VMEM((slots, rows, width), BF16),
            pltpu.VMEM((slots, rows, width), BF16),
            pltpu.VMEM((slots, rows, width), BF16),
            pltpu.VMEM((slots, rows, width), BF16),
            pltpu.VMEM((groups, slots, rows), BF16),
            pltpu.VMEM((groups, slots, rows), BF16),
            pltpu.VMEM((groups, slots), jnp.int32),
            pltpu.VMEM((groups, slots), jnp.int32),
            pltpu.VMEM((1, ecorr.shape[0]), F32),
            pltpu.SMEM((groups, slots), jnp.int32),
            *[pltpu.VMEM((slots + 1, 2, hw, hw), F32)] * groups,
            *[pltpu.VMEM((slots + 1, 8, hw), F32)] * groups,
            pltpu.VMEM((groups * slots, 8, rows), F32),
            *[pltpu.VMEM((slots, 8, width), F32)] * groups,
            pltpu.VMEM((2 * PG, 2, hw, hw), BF16),
            pltpu.VMEM((2 * PG, 2, hw, hw), BF16),
            pltpu.VMEM((PG, 2, hw, hw), BF16),
            pltpu.VMEM((PG, hw, hw), BF16),
            pltpu.VMEM((PG, 3, hw, hw), BF16),
            pltpu.VMEM((PG, nz, 2, share, hw), BF16),
            pltpu.VMEM((PG, nz, 2, share, hw), BF16),
            pltpu.VMEM((HOPS, 2, share, hw), F32),
            pltpu.VMEM((HOPS, share, hw), BF16),
            pltpu.VMEM((HOPS, share, hw), BF16),
            pltpu.VMEM((2,) + tile, F32),
            pltpu.VMEM((2,) + tile, F32),
            pltpu.VMEM(tile, F32),
            pltpu.VMEM(tile, F32),
            pltpu.VMEM((3,) + tile, F32),
            pltpu.VMEM(tile, F32),
            pltpu.VMEM((nz - 1,) + tile[1:], F32),
            pltpu.SemaphoreType.DMA((8,)),
            pltpu.SemaphoreType.DMA((5,)),
            pltpu.SemaphoreType.DMA((n_arrivals,)),
        ],
        compiler_params=pltpu.CompilerParams(
            collective_id=0, has_side_effects=True
        ),
    )(basis[0], residual[0], sigma[0], counts[0], pulsar[0], ecorr.reshape(1, -1))
    return pl.pallas_call(
        functools.partial(scale_kernel, norm_rows, all_rows),
        out_shape=(
            jax.ShapeDtypeStruct((PG, share, width), F32),
            jax.ShapeDtypeStruct((PG, share), F32),
            jax.ShapeDtypeStruct((2,), F32),
        ),
        in_specs=[vmem] * 3,
        out_specs=(vmem, vmem, pl.BlockSpec(memory_space=pltpu.SMEM)),
    )(*[pltpu.with_memory_space_constraint(a, pltpu.VMEM) for a in sums])


def slot_terms(basis, residual, sigma, counts, pulsar, group_ids, ecorr):
    sig = sigma.astype(jnp.float32)
    res = residual.astype(jnp.float32)
    rowpos = lax.broadcasted_iota(jnp.int32, sig.shape, 2)
    valid = rowpos < counts[..., None]
    inverse = jnp.where(valid, 1.0 / (sig * sig), jnp.float32(0.0))
    weighted = (inverse[..., None] * basis).astype(jnp.bfloat16)
    global_id = group_ids[:, None] * PG + pulsar
    table = jnp.arange(ecorr.shape[0], dtype=jnp.int32)
    chosen = jnp.sum(jnp.where(global_id[..., None] == table, ecorr, jnp.float32(0.0)), axis=-1)
    jitter = chosen * chosen
    total = jnp.sum(inverse, axis=2)
    coef = jitter / (1.0 + jitter * total)
    column = jnp.sum(weighted.astype(jnp.float32), axis=2)
    project = jnp.sum(weighted.astype(jnp.float32) * res[..., None], axis=2)
    wsum = jnp.sum(inverse * res, axis=2)
    chi = jnp.sum(inverse * res * res) - jnp.sum(coef * wsum * wsum)
    logdet = jnp.sum(jnp.where(valid, jnp.log(sig * sig), jnp.float32(0.0))) + jnp.sum(
        jnp.log(1.0 + jitter * total)
    )
    adjusted = project - (coef * wsum)[..., None] * column
    grams = []
    sums = []
    for member in range(PG):
        picked = pulsar == member
        masked = jnp.where(picked[..., None, None], weighted, jnp.zeros((), jnp.bfloat16))
        first = jnp.einsum("gslk,gslm->gkm", basis, masked, preferred_element_type=jnp.float32)
        scale = jnp.where(picked, coef, jnp.float32(0.0))
        minus = jnp.einsum(
            "gs,gsk,gsm->gkm", scale, column, column, precision=lax.Precision.HIGHEST
        )
        grams.append(first - minus)
        sums.append(jnp.sum(jnp.where(picked[..., None], adjusted, jnp.float32(0.0)), axis=1))
    return (jnp.stack(grams, axis=1), jnp.stack(sums, axis=1), logdet, chi)


def on_device(basis, residual, sigma, counts, pulsar, ecorr):
    groups = lax.axis_size("psr")
    ndp = lax.axis_size("dp")
    width = basis.shape[-1]
    rows = basis.shape[-2]
    slots = basis.shape[2]
    share = width // ndp
    group_ids = jnp.arange(groups, dtype=jnp.int32)
    gram, rhs, logdet, chi = slot_terms(
        basis[0], residual[0], sigma[0], counts[0], pulsar[0], group_ids, ecorr
    )
    gram_rows = (
        gram.reshape(groups, PG, ndp, share, width)
        .transpose(2, 0, 1, 3, 4)
        .reshape(ndp * groups * PG * share, width)
    )
    rhs_rows = (
        rhs.reshape(groups, PG, ndp, share).transpose(2, 0, 1, 3).reshape(ndp * groups * PG * share)
    )
    gram_part, rhs_part = (
        lax.psum_scatter(gram_rows, ("dp", "psr"), scatter_dimension=0, tiled=True),
        lax.psum_scatter(rhs_rows, ("dp", "psr"), scatter_dimension=0, tiled=True),
    )
    gram_part = gram_part.reshape(PG, share, width)
    rhs_part = rhs_part.reshape(PG, share)
    summed = lax.psum((logdet, chi), ("dp", "psr"))
    norm_rows = float(ndp * slots * rows)
    all_rows = float(ndp * groups * groups * slots * rows)
    totals = jnp.stack([summed[0], summed[1]]) / all_rows
    return (gram_part / norm_rows, rhs_part / norm_rows, totals)


def solution(mesh):
    def step(basis, *rest):
        groups, _, rows, width = basis.shape[1:]
        ndp = lax.axis_size("dp")
        tiled = ndp % 4 == 0 and width % (16 * ndp) == 0 and width % 256 == 0 and width == 2 * rows
        if groups == lax.axis_size("psr") == 2 * 2 and tiled:
            return fused(basis, *rest)
        return on_device(basis, *rest)

    return jax.shard_map(
        step,
        mesh=mesh,
        in_specs=(
            P(("dp", "psr"), None, None, None, None),
            P(("dp", "psr"), None, None, None),
            P(("dp", "psr"), None, None, None),
            P(("dp", "psr"), None, None),
            P(("dp", "psr"), None, None),
            P(),
        ),
        out_specs=(P("psr", "dp", None), P("psr", "dp"), P()),
        check_vma=False,
    )
```
